32 devices in a mesh: group: 2 (over y), region: 4 (over z), probe: 4 (over x, core).
Axes of the slice: x: 2, y: 2, z: 4, core: 2. Of those that a mesh axis runs over, the one named last changes fastest.
Arguments:
- object_slices: float32 [4, 2, 512, 256], P('group', None, 'region', 'probe'), parts along dimension 0, may hold values from -4 to 4
- probe: float32 [4, 128, 128], P('group'), parts along dimension 0, may hold values from -6 to 6
- intensity: float32 [4, 16, 256, 128], P('region', 'probe', 'group'), parts along dimension 2, may hold values from 0.5 to 4
- positions: int32 [4, 16, 4], P('region', 'probe', 'group'), parts along dimension 2, may hold values from 0 to 255, as said below
Outputs:
- gradient: float32 [4, 2, 512, 256], P('group', None, 'region', 'probe'), parts along dimension 0
The draws below stay inside these ranges and needn't reach their ends.
There are 2 independent parts, one for each index of `group`. The reference program is written for one: setup_inputs(seed, part) draws one part's arguments, and reference() takes and returns one part's arrays. A program takes and returns all parts, laid end to end along the dimension named above; each array names one. Nothing has to cross between parts.
Inputs may be any that keep to these rules, and one draw needn't show every extreme that they name: `positions`: entry 0 is a row offset below 128 within the region's rows, entry 1 a column offset below 256.
All inputs are finite; a program needn't handle non-finite values.
Results may differ from the reference program's by a relative error of at most 0.00014.
Values sent between devices are 32-bit elements; how exact they have to be, the bound alone decides.
No kernel may reach another device: no remote copies, remote signals or barrier semaphores. Data moves between devices by JAX's collectives and lax.ppermute only.
A program may use at most 64 MiB of HBM per device.

```python
import jax
import jax.numpy as jnp

WINDOW = 128
SLICES = 2
BAND = 128
REGIONS = 4
REGION_POS = 16
ROWS = 512
COLUMNS = 256


def draw_positions(key, part):
    first_key, second_key = jax.random.split(key)
    row_offsets = jax.random.randint(first_key, (REGIONS, REGION_POS), 0, BAND, dtype=jnp.int32)
    col_offsets = jax.random.randint(second_key, (REGIONS, REGION_POS), 0, COLUMNS, dtype=jnp.int32)
    stacked = jnp.stack([row_offsets, col_offsets], axis=-1)
    stacked = stacked.at[0, 0].set(jnp.array([BAND - 1, COLUMNS - 1], jnp.int32))
    stacked = stacked.at[0, 1].set(jnp.zeros((2,), jnp.int32))
    return stacked


def shard_levels(stream_key, shape, shards, smallest, high):
    def one(axis_at, blocks):
        heights = jax.random.uniform(jax.random.fold_in(jax.random.fold_in(stream_key, 6), axis_at), (blocks,), jnp.float32, smallest / len(shards), high / len(shards))
        return jnp.repeat(jnp.exp(heights), shape[axis_at] // blocks).reshape((-1,) + (1,) * (len(shape) - axis_at - 1))

    gain = one(*shards[0])
    for cut in shards[1:]:
        gain = gain * one(*cut)
    return gain


def scatter_about(rng, dims, spread, limit, shards=(), held_as=jnp.bfloat16):
    values = jax.random.normal(rng, dims, jnp.float32) * spread
    if len(shards) > 0:
        values = shard_levels(rng, dims, shards, -0.22, 0.18) * values
    return jnp.clip(values, min=-limit, max=limit).astype(held_as)


def setup_inputs(seed: int = 0, part: int = 0) -> dict:
    arg_keys = jax.random.split(jax.random.key(seed), 5)
    own_keys = jax.random.split(jax.random.fold_in(arg_keys[4], part), 5)
    object_slices = scatter_about(own_keys[0], (SLICES, 2, ROWS, COLUMNS), 0.7, 4.0, ((2, 4), (3, 4)), jnp.float32)
    probe = scatter_about(own_keys[1], (2, WINDOW, WINDOW), 1.0, 6.0, (), jnp.float32)
    intensity = jnp.clip(0.5 + 3.5 * jax.random.uniform(own_keys[2], (REGIONS, REGION_POS, WINDOW, WINDOW), jnp.float32) ** shard_levels(own_keys[2], (REGIONS, REGION_POS, WINDOW, WINDOW), ((0, 4), (1, 4)), -0.2, 0.2), 0.5, 4.0)
    positions = draw_positions(jax.random.fold_in(jax.random.fold_in(arg_keys[4], part), 71), part)
    return {"object_slices": object_slices, "probe": probe, "intensity": intensity, "positions": positions}


def propagator(window):
    indices = jnp.arange(window, dtype=jnp.int32)
    frequency = jnp.where(indices < window // 2, indices, indices - window).astype(jnp.float32) / window
    phases = -60.0 * (frequency[:, None] ** 2 + frequency[None, :] ** 2)
    return jnp.cos(phases), jnp.sin(phases)


def reference(object_slices, probe, intensity, positions):
    object_field = object_slices[:, 0] + 1j * object_slices[:, 1]
    probe_wave = probe[0] + 1j * probe[1]
    kernel_re, kernel_im = propagator(WINDOW)
    kernel = kernel_re + 1j * kernel_im
    offsets = jnp.arange(WINDOW, dtype=jnp.int32)
    gradient = jnp.zeros(object_field.shape, object_field.dtype)
    for region in range(REGIONS):
        row_index = (region * BAND + positions[region, :, 0][:, None] + offsets[None, :]) % ROWS
        col_index = (positions[region, :, 1][:, None] + offsets[None, :]) % COLUMNS
        patches = object_field[:, row_index[:, :, None], col_index[:, None, :]]
        incoming = jnp.broadcast_to(probe_wave, patches.shape[1:])
        waves_in = []
        exit_wave = incoming
        for layer in range(SLICES):
            waves_in.append(incoming)
            exit_wave = incoming * patches[layer]
            if layer < SLICES - 1:
                incoming = jnp.fft.ifft2(kernel * jnp.fft.fft2(exit_wave, norm="ortho"), norm="ortho")
        far_field = jnp.fft.fft2(exit_wave, norm="ortho")
        misfit = far_field.real ** 2 + far_field.imag ** 2 - intensity[region]
        returned = jnp.fft.ifft2(misfit * far_field, norm="ortho")
        layer_grads = [None] * SLICES
        for layer in reversed(range(SLICES)):
            layer_grads[layer] = jnp.conj(waves_in[layer]) * returned
            if layer > 0:
                moved = jnp.fft.fft2(jnp.conj(patches[layer]) * returned, norm="ortho")
                returned = jnp.fft.ifft2(jnp.conj(kernel) * moved, norm="ortho")
        gradient = gradient.at[:, row_index[:, :, None], col_index[:, None, :]].add(jnp.stack(layer_grads))
    gradient = gradient / REGION_POS
    return jnp.stack([gradient.real, gradient.imag], axis=1).astype(jnp.float32)
```

```python
import math

import jax
import jax.numpy as jnp
import ml_dtypes
import numpy as np
from jax import lax
from jax.experimental import pallas as pl
from jax.experimental.pallas import tpu as pltpu
from jax.sharding import PartitionSpec as P

CORES = 2
HALF = 64


def split_table(table):
    high = table.astype(ml_dtypes.bfloat16)
    low = (table - high.astype(np.float64)).astype(ml_dtypes.bfloat16)
    return np.stack([high, low])


def tables(window):
    indices = np.arange(window)
    angles = 2.0 * math.pi * ((indices[:, None] * indices[None, :]) % window) / window
    real, imag = np.cos(angles) / math.sqrt(window), -np.sin(angles) / math.sqrt(window)
    direct = np.block([[real, imag], [-imag, real]])
    inverse = np.block([[real, -imag], [imag, real]])
    frequency = np.where(indices < window // 2, indices, indices - window) / window
    phases = -60.0 * (frequency[:, None] ** 2 + frequency[None, :] ** 2)
    kernel = np.stack([np.cos(phases), np.sin(phases)]).astype(np.float32)
    return split_table(direct), split_table(inverse), kernel


def split(values):
    high = values.astype(jnp.bfloat16)
    low = (values - high.astype(jnp.float32)).astype(jnp.bfloat16)
    return high, low


def times_right(values, table_ref):
    high, low = split(values)
    table = jnp.concatenate([table_ref[0], table_ref[0], table_ref[1]], axis=0)
    stacked = jnp.concatenate([high, low, high], axis=1)
    return jnp.dot(stacked, table, preferred_element_type=jnp.float32)


def times_left(table_ref, values):
    high, low = split(values)
    table = jnp.concatenate([table_ref[0], table_ref[0], table_ref[1]], axis=1)
    stacked = jnp.concatenate([high, low, high], axis=0)
    return jnp.dot(table, stacked, preferred_element_type=jnp.float32)


def to_rows(values, window):
    count = values.shape[0] // window
    return jnp.concatenate(
        [
            jnp.concatenate(
                [values[n * window : (n + 1) * window, c * window : (c + 1) * window] for n in range(count)],
                axis=1,
            )
            for c in range(2)
        ],
        axis=0,
    )


def part(values, n, c, window):
    return values[c * window : (c + 1) * window, n * window : (n + 1) * window]


def join(pairs):
    return jnp.concatenate(
        [jnp.concatenate([re for re, _ in pairs], axis=1), jnp.concatenate([im for _, im in pairs], axis=1)],
        axis=0,
    )


def lanes(pairs):
    return jnp.concatenate([jnp.concatenate([re, im], axis=1) for re, im in pairs], axis=0)


def fresnel(pairs, direct_ref, inverse_ref, kernel_ref, sign, window):
    count = len(pairs)
    half = to_rows(times_right(lanes(pairs), direct_ref), window)
    spec = times_left(inverse_ref, half)
    k_re, k_im = kernel_ref[0], kernel_ref[1]
    if sign < 0:
        k_im = -k_im
    moved = []
    for n in range(count):
        re, im = part(spec, n, 0, window), part(spec, n, 1, window)
        moved.append((k_re * re - k_im * im, k_re * im + k_im * re))
    half = to_rows(times_right(lanes(moved), inverse_ref), window)
    wave = times_left(direct_ref, half)
    return [(part(wave, n, 0, window), part(wave, n, 1, window)) for n in range(count)]


def assemble(unit_refs, field_ref, ring, rows, window):
    me = lax.axis_index("probe")
    x, core = me // CORES, me % CORES
    lane = lax.broadcasted_iota(jnp.int32, (rows, window), 1)
    at = 0
    for step in range(ring):
        tile = lax.rem(x + step, ring)
        for band in range(2):
            mine, other = unit_refs[at][...], unit_refs[at + 1][...]
            at += 2
            even = jnp.where(core == 0, mine, other)
            odd = jnp.where(core == 0, other, mine)
            where = pl.ds(band * rows, rows)
            field_ref[tile, 0, where, :] = jnp.where(lane < HALF, even, pltpu.roll(odd, HALF, 1))
            field_ref[tile, 1, where, :] = jnp.where(lane < HALF, pltpu.roll(even, HALF, 1), odd)


def cut(field_ref, position_ref, n, ring, window):
    row, column = position_ref[0, n, 0], position_ref[0, n, 1]
    tile = column // window
    after = jnp.where(tile + 1 == ring, 0, tile + 1)
    offset = column - tile * window
    back = lax.rem(window - offset, window)
    lane = lax.broadcasted_iota(jnp.int32, (window, window), 1)
    halves = []
    for c in range(2):
        first = pltpu.roll(field_ref[tile, c, pl.ds(row, window), :], back, 1)
        second = pltpu.roll(field_ref[after, c, pl.ds(row, window), :], back, 1)
        halves.append(jnp.where(lane < window - offset, first, second))
    return tuple(halves)


def deposit(total_ref, position_ref, n, pair, ring, window):
    row, column = position_ref[0, n, 0], position_ref[0, n, 1]
    tile = column // window
    after = jnp.where(tile + 1 == ring, 0, tile + 1)
    offset = column - tile * window
    lane = lax.broadcasted_iota(jnp.int32, (window, window), 1)
    rows = pl.ds(row, window)
    for c in range(2):
        turned = pltpu.roll(pair[c], offset, 1)
        total_ref[tile, c, rows, :] += jnp.where(lane >= offset, turned, 0.0)
        total_ref[after, c, rows, :] += jnp.where(lane < offset, turned, 0.0)


def hand_out(total_ref, keep_ref, send_ref, ring, rows, window):
    me = lax.axis_index("probe")
    x, core = me // CORES, me % CORES
    lane = lax.broadcasted_iota(jnp.int32, (rows, window), 1)
    for step in range(ring):
        tile = lax.rem(x + step, ring)
        for band in range(2):
            where = pl.ds(band * rows, rows)
            re, im = total_ref[tile, 0, where, :], total_ref[tile, 1, where, :]
            even = jnp.where(lane < HALF, re, pltpu.roll(im, HALF, 1))
            odd = jnp.where(lane < HALF, pltpu.roll(re, HALF, 1), im)
            keep_ref[2 * step + band] = jnp.where(core == 0, even, odd)
            send_ref[2 * step + band] = jnp.where(core == 0, odd, even)


def pack_kernel(object_ref, *out_refs):
    for layer, out_ref in enumerate(out_refs):
        out_ref[...] = jnp.concatenate([object_ref[layer, 0], object_ref[layer, 1]], axis=1)


def first_kernel(ring, rows, window, position_ref, probe_ref, direct_ref, inverse_ref, kernel_ref, *rest):
    unit_refs, wave_ref, field_ref = rest[:-2], rest[-2], rest[-1]
    count = position_ref.shape[1]
    assemble(unit_refs, field_ref, ring, rows, window)
    probe_re, probe_im = probe_ref[0], probe_ref[1]
    exits = []
    for n in range(count):
        re, im = cut(field_ref, position_ref, n, ring, window)
        exits.append((probe_re * re - probe_im * im, probe_re * im + probe_im * re))
    waves = fresnel(exits, direct_ref, inverse_ref, kernel_ref, 1, window)
    for n, (re, im) in enumerate(waves):
        wave_ref[n, 0] = re
        wave_ref[n, 1] = im


def middle_kernel(ring, rows, window, position_ref, wave_ref, intensity_ref, direct_ref, inverse_ref, *rest):
    unit_refs, (carried_ref, keep_ref, send_ref, field_ref, total_ref) = rest[:-5], rest[-5:]
    count = position_ref.shape[1]
    assemble(unit_refs, field_ref, ring, rows, window)
    total_ref[...] = jnp.zeros_like(total_ref)
    exits, patches = [], []
    for n in range(count):
        re, im = cut(field_ref, position_ref, n, ring, window)
        w_re, w_im = wave_ref[n, 0], wave_ref[n, 1]
        patches.append((re, im))
        exits.append((w_re * re - w_im * im, w_re * im + w_im * re))
    far = times_left(inverse_ref, to_rows(times_right(lanes(exits), direct_ref), window))
    scaled = []
    for n in range(count):
        re, im = part(far, n, 0, window), part(far, n, 1, window)
        misfit = re * re + im * im - intensity_ref[0, n]
        scaled.append((misfit * re, misfit * im))
    back = times_left(direct_ref, to_rows(times_right(lanes(scaled), inverse_ref), window))
    for n in range(count):
        b_re, b_im = part(back, n, 0, window), part(back, n, 1, window)
        w_re, w_im = wave_ref[n, 0], wave_ref[n, 1]
        p_re, p_im = patches[n]
        carried_ref[n, 0] = p_re * b_re + p_im * b_im
        carried_ref[n, 1] = p_re * b_im - p_im * b_re
        gradient = (w_re * b_re + w_im * b_im, w_re * b_im - w_im * b_re)
        deposit(total_ref, position_ref, n, gradient, ring, window)
    hand_out(total_ref, keep_ref, send_ref, ring, rows, window)


def last_kernel(
    ring, rows, window, position_ref, probe_ref, carried_ref, direct_ref, inverse_ref, kernel_ref, keep_ref, send_ref, total_ref
):
    count = position_ref.shape[1]
    total_ref[...] = jnp.zeros_like(total_ref)
    carried = [(carried_ref[n, 0], carried_ref[n, 1]) for n in range(count)]
    backs = fresnel(carried, direct_ref, inverse_ref, kernel_ref, -1, window)
    probe_re, probe_im = probe_ref[0], probe_ref[1]
    for n, (b_re, b_im) in enumerate(backs):
        gradient = (probe_re * b_re + probe_im * b_im, probe_re * b_im - probe_im * b_re)
        deposit(total_ref, position_ref, n, gradient, ring, window)
    hand_out(total_ref, keep_ref, send_ref, ring, rows, window)


def sum_kernel(scale, per_layer, *refs):
    out_ref = refs[-1]
    for layer in range(out_ref.shape[0]):
        terms = refs[layer * per_layer : (layer + 1) * per_layer]
        total = terms[0][...]
        for term in terms[1:]:
            total += term[...]
        total *= scale
        out_ref[layer, 0] = total[:, :HALF]
        out_ref[layer, 1] = total[:, HALF:]


VMEM = pl.BlockSpec(memory_space=pltpu.VMEM)
SMEM = pl.BlockSpec(memory_space=pltpu.SMEM)
PARAMS = pltpu.CompilerParams(vmem_limit_bytes=40 << 20)


def cost(flops, moved):
    return pl.CostEstimate(flops=flops, bytes_accessed=moved, transcendentals=0)


def body(object_slices, probe, intensity, positions):
    layers, _, rows, _ = object_slices.shape
    window = probe.shape[1]
    count = positions.shape[1]
    regions = lax.axis_size("region")
    devices = lax.axis_size("probe")
    ring = devices // CORES
    direct, inverse, kernel = (jnp.asarray(t) for t in tables(window))
    unit = jax.ShapeDtypeStruct((rows, window), jnp.float32)
    waves = jax.ShapeDtypeStruct((count, 2, window, window), jnp.float32)
    units = jax.ShapeDtypeStruct((2 * ring, rows, window), jnp.float32)
    field = pltpu.VMEM((ring, 2, 2 * rows, window), jnp.float32)
    dft_flops = count * 2 * 3 * 2 * window * (2 * window) ** 2

    def swap(value):
        return lax.ppermute(value, "probe", [(i, i ^ 1) for i in range(devices)])

    def route(step, band):
        pairs = []
        for r in range(regions):
            for d in range(devices):
                there = ((d // CORES + step) % ring) * CORES + d % CORES
                pairs.append((r * devices + d, ((r + band) % regions) * devices + there))
        return pairs

    def fetch(value, step, band):
        return lax.ppermute(value, ("region", "probe"), [(b, a) for a, b in route(step, band)])

    def give(value, step, band):
        return lax.ppermute(value, ("region", "probe"), route(step, band))

    steps = [(step, band) for step in range(ring) for band in range(2)]

    def gathered(tile):
        out = []
        for step, band in steps:
            here = tile if step == band == 0 else fetch(tile, step, band)
            out += [here, swap(here)]
        return out

    packed = pl.pallas_call(
        pack_kernel, out_shape=[unit] * layers, in_specs=[VMEM], out_specs=[VMEM] * layers, compiler_params=PARAMS
    )(object_slices)
    unit_sets = [gathered(tile) for tile in packed]
    wave = pl.pallas_call(
        lambda *refs: first_kernel(ring, rows, window, *refs),
        out_shape=waves,
        in_specs=[SMEM] + [VMEM] * (4 + 4 * ring),
        out_specs=VMEM,
        scratch_shapes=[field],
        compiler_params=PARAMS,
        cost_estimate=cost(2 * dft_flops, 1 << 20),
    )(positions, probe, direct, inverse, kernel, *unit_sets[0])
    carried, keep_1, send_1 = pl.pallas_call(
        lambda *refs: middle_kernel(ring, rows, window, *refs),
        out_shape=[waves, units, units],
        in_specs=[SMEM] + [VMEM] * (4 + 4 * ring),
        out_specs=[VMEM] * 3,
        scratch_shapes=[field, field],
        compiler_params=PARAMS,
        cost_estimate=cost(2 * dft_flops, 1 << 20),
    )(positions, wave, intensity, direct, inverse, *unit_sets[1])
    keep_0, send_0 = pl.pallas_call(
        lambda *refs: last_kernel(ring, rows, window, *refs),
        out_shape=[units, units],
        in_specs=[SMEM] + [VMEM] * 5,
        out_specs=[VMEM] * 2,
        scratch_shapes=[field],
        compiler_params=PARAMS,
        cost_estimate=cost(2 * dft_flops, 1 << 20),
    )(positions, probe, carried, direct, inverse, kernel)

    def returned(keep, send):
        other = swap(send)
        out = []
        for at, (step, band) in enumerate(steps):
            both = keep[at] + other[at]
            out.append(both if at == 0 else give(both, step, band))
        return out

    terms_1 = returned(keep_1, send_1)
    terms_0 = returned(keep_0, send_0)
    return pl.pallas_call(
        lambda *refs: sum_kernel(1.0 / (count * devices), 2 * ring, *refs),
        out_shape=jax.ShapeDtypeStruct(object_slices.shape, jnp.float32),
        in_specs=[VMEM] * (4 * ring),
        out_specs=VMEM,
        compiler_params=PARAMS,
    )(*terms_0, *terms_1)


def solution(mesh):
    placed = (
        P("group", None, "region", "probe"),
        P("group", None, None),
        P("region", "probe", "group", None),
        P("region", "probe", "group"),
    )
    return jax.shard_map(
        body,
        mesh=mesh,
        in_specs=placed,
        out_specs=P("group", None, "region", "probe"),
        check_vma=False,
    )
```

```python
import math

import jax
import jax.numpy as jnp
import ml_dtypes
import numpy as np
from jax import lax
from jax.experimental import pallas as pl
from jax.experimental.pallas import tpu as pltpu
from jax.sharding import PartitionSpec as P

CORES = 2
HALF = 64


def split_table(table):
    high = table.astype(ml_dtypes.bfloat16)
    low = (table - high.astype(np.float64)).astype(ml_dtypes.bfloat16)
    return np.stack([high, low])


def tables(window):
    indices = np.arange(window)
    angles = 2.0 * math.pi * ((indices[:, None] * indices[None, :]) % window) / window
    real, imag = np.cos(angles) / math.sqrt(window), -np.sin(angles) / math.sqrt(window)
    direct = np.block([[real, imag], [-imag, real]])
    inverse = np.block([[real, -imag], [imag, real]])
    frequency = np.where(indices < window // 2, indices, indices - window) / window
    phases = -60.0 * (frequency[:, None] ** 2 + frequency[None, :] ** 2)
    kernel = np.stack([np.cos(phases), np.sin(phases)]).astype(np.float32)
    return split_table(direct), split_table(inverse), kernel


def split(values):
    high = values.astype(jnp.bfloat16)
    low = (values - high.astype(jnp.float32)).astype(jnp.bfloat16)
    return high, low


def times_right(values, table_ref):
    high, low = split(values)
    table = jnp.concatenate([table_ref[0], table_ref[0], table_ref[1]], axis=0)
    stacked = jnp.concatenate([high, low, high], axis=1)
    return jnp.dot(stacked, table, preferred_element_type=jnp.float32)


def times_left(table_ref, values):
    high, low = split(values)
    table = jnp.concatenate([table_ref[0], table_ref[0], table_ref[1]], axis=1)
    stacked = jnp.concatenate([high, low, high], axis=0)
    return jnp.dot(table, stacked, preferred_element_type=jnp.float32)


def to_rows(values, window):
    count = values.shape[0] // window
    return jnp.concatenate(
        [
            jnp.concatenate(
                [values[n * window : (n + 1) * window, c * window : (c + 1) * window] for n in range(count)],
                axis=1,
            )
            for c in range(2)
        ],
        axis=0,
    )


def part(values, n, c, window):
    return values[c * window : (c + 1) * window, n * window : (n + 1) * window]


def join(pairs):
    return jnp.concatenate(
        [jnp.concatenate([re for re, _ in pairs], axis=1), jnp.concatenate([im for _, im in pairs], axis=1)],
        axis=0,
    )


def lanes(pairs):
    return jnp.concatenate([jnp.concatenate([re, im], axis=1) for re, im in pairs], axis=0)


def fresnel(pairs, direct_ref, inverse_ref, kernel_ref, sign, window):
    count = len(pairs)
    half = to_rows(times_right(lanes(pairs), direct_ref), window)
    spec = times_left(inverse_ref, half)
    k_re, k_im = kernel_ref[0], kernel_ref[1]
    if sign < 0:
        k_im = -k_im
    moved = []
    for n in range(count):
        re, im = part(spec, n, 0, window), part(spec, n, 1, window)
        moved.append((k_re * re - k_im * im, k_re * im + k_im * re))
    half = to_rows(times_right(lanes(moved), inverse_ref), window)
    wave = times_left(direct_ref, half)
    return [(part(wave, n, 0, window), part(wave, n, 1, window)) for n in range(count)]


def travel_order(ring):
    return [(0, 0)] + [(step, band) for band in range(2) for step in range(ring - 1, -1, -1) if step or band]


def assemble(unit_refs, field_ref, ring, window):
    me = lax.axis_index("probe")
    x, core = me // CORES, me % CORES
    layers = field_ref.shape[0]
    columns = field_ref.shape[3] - window
    at = 0
    for step, band in travel_order(ring):
        tile = lax.rem(x + step, ring)
        for owner in (core, 1 - core):
            where = pl.ds(pl.multiple_of((tile * CORES + owner) * HALF, HALF), HALF)
            for layer in range(layers):
                for c in range(2):
                    field_ref[layer, c, band, where, :] = unit_refs[at][layer, c]
            at += 1
    field_ref[:, :, :, columns:, :] = field_ref[:, :, :, :window, :]


def cut(field_ref, layer, position_ref, n, window):
    row, column = position_ref[0, n, 0], position_ref[0, n, 1]
    back = lax.rem(window - row, window)
    lane = lax.broadcasted_iota(jnp.int32, (window, window), 1)
    halves = []
    for c in range(2):
        first = pltpu.roll(field_ref[layer, c, 0, pl.ds(column, window), :], back, 1)
        second = pltpu.roll(field_ref[layer, c, 1, pl.ds(column, window), :], back, 1)
        halves.append(jnp.where(lane < window - row, first, second))
    return tuple(halves)


def deposit(total_ref, position_ref, n, pair, window):
    row, column = position_ref[0, n, 0], position_ref[0, n, 1]
    lane = lax.broadcasted_iota(jnp.int32, (window, window), 1)
    where = pl.ds(column, window)
    for c in range(2):
        turned = pltpu.roll(pair[c], row, 1)
        total_ref[c, 0, where, :] += jnp.where(lane >= row, turned, 0.0)
        total_ref[c, 1, where, :] += jnp.where(lane < row, turned, 0.0)


def hand_out(total_ref, keep_ref, send_ref, ring, window):
    me = lax.axis_index("probe")
    x, core = me // CORES, me % CORES
    columns = total_ref.shape[2] - window
    total_ref[:, :, :window, :] += total_ref[:, :, columns:, :]
    for at, (step, band) in enumerate(travel_order(ring)):
        tile = lax.rem(x + step, ring)
        for owner, ref in ((core, keep_ref), (1 - core, send_ref)):
            where = pl.ds(pl.multiple_of((tile * CORES + owner) * HALF, HALF), HALF)
            for c in range(2):
                ref[at, c] = total_ref[c, band, where, :]


def prepare_kernel(*refs):
    sources, outputs = refs[:5], refs[5:10]
    probe_ref, intensity_ref, sems = refs[10:]
    targets = (probe_ref, intensity_ref) + outputs[2:]
    copies = [pltpu.make_async_copy(a, b, sems.at[i]) for i, (a, b) in enumerate(zip(sources, targets))]
    for copy in copies:
        copy.start()
    copies[0].wait()
    for c in range(2):
        outputs[0][c] = probe_ref[c].T
    copies[1].wait()
    for n in range(intensity_ref.shape[1]):
        outputs[1][n] = intensity_ref[0, n].T
    for copy in copies[2:]:
        copy.wait()


def main_kernel(ring, window, position_ref, probe_ref, intensity_ref, direct_ref, inverse_ref, kernel_ref, *rest):
    unit_refs, (carried_ref, keep_ref, send_ref, field_ref, wave_ref, total_ref) = rest[:-6], rest[-6:]
    count = position_ref.shape[1]
    assemble(unit_refs, field_ref, ring, window)
    total_ref[...] = jnp.zeros_like(total_ref)
    probe_re, probe_im = probe_ref[0], probe_ref[1]
    exits = []
    for n in range(count):
        re, im = cut(field_ref, 0, position_ref, n, window)
        exits.append((probe_re * re - probe_im * im, probe_re * im + probe_im * re))
    waves = fresnel(exits, direct_ref, inverse_ref, kernel_ref, 1, window)
    exits, patches = [], []
    for n in range(count):
        re, im = cut(field_ref, 1, position_ref, n, window)
        w_re, w_im = waves[n]
        wave_ref[n, 0] = w_re
        wave_ref[n, 1] = w_im
        exits.append((w_re * re - w_im * im, w_re * im + w_im * re))
    far = times_left(inverse_ref, to_rows(times_right(lanes(exits), direct_ref), window))
    scaled = []
    for n in range(count):
        re, im = part(far, n, 0, window), part(far, n, 1, window)
        misfit = re * re + im * im - intensity_ref[n]
        scaled.append((misfit * re, misfit * im))
    back = times_left(direct_ref, to_rows(times_right(lanes(scaled), inverse_ref), window))
    for n in range(count):
        b_re, b_im = part(back, n, 0, window), part(back, n, 1, window)
        w_re, w_im = wave_ref[n, 0], wave_ref[n, 1]
        p_re, p_im = cut(field_ref, 1, position_ref, n, window)
        carried_ref[n, 0] = p_re * b_re + p_im * b_im
        carried_ref[n, 1] = p_re * b_im - p_im * b_re
        gradient = (w_re * b_re + w_im * b_im, w_re * b_im - w_im * b_re)
        deposit(total_ref, position_ref, n, gradient, window)
    hand_out(total_ref, keep_ref, send_ref, ring, window)


def last_kernel(
    ring, window, position_ref, probe_ref, carried_ref, direct_ref, inverse_ref, kernel_ref, keep_ref, send_ref, total_ref
):
    count = position_ref.shape[1]
    total_ref[...] = jnp.zeros_like(total_ref)
    carried = [(carried_ref[n, 0], carried_ref[n, 1]) for n in range(count)]
    backs = fresnel(carried, direct_ref, inverse_ref, kernel_ref, -1, window)
    probe_re, probe_im = probe_ref[0], probe_ref[1]
    for n, (b_re, b_im) in enumerate(backs):
        gradient = (probe_re * b_re + probe_im * b_im, probe_re * b_im - probe_im * b_re)
        deposit(total_ref, position_ref, n, gradient, window)
    hand_out(total_ref, keep_ref, send_ref, ring, window)


def pair_kernel(layers, *refs):
    inputs, outputs = refs[: 2 * layers], refs[2 * layers :]
    for layer in range(layers):
        for at, out_ref in enumerate(outputs):
            out_ref[layer] = inputs[2 * layer][at] + inputs[2 * layer + 1][at]


def sum_kernel(scale, *refs):
    total = refs[0][...]
    for ref in refs[1:-1]:
        total += ref[...]
    refs[-1][...] = total * scale


VMEM = pl.BlockSpec(memory_space=pltpu.VMEM)
HBM = pl.BlockSpec(memory_space=pltpu.HBM)
SMEM = pl.BlockSpec(memory_space=pltpu.SMEM)
PARAMS = pltpu.CompilerParams(vmem_limit_bytes=40 << 20)


def cost(flops, moved):
    return pl.CostEstimate(flops=flops, bytes_accessed=moved, transcendentals=0)


def body(object_slices, probe, intensity, positions):
    layers, _, rows, width = object_slices.shape
    window = probe.shape[1]
    count = positions.shape[1]
    regions = lax.axis_size("region")
    devices = lax.axis_size("probe")
    ring = devices // CORES
    columns = devices * width
    direct, inverse, kernel = (jnp.asarray(t) for t in tables(window))
    unit = jax.ShapeDtypeStruct((layers, 2, width, rows), jnp.float32)
    waves = jax.ShapeDtypeStruct((count, 2, window, window), jnp.float32)
    units = jax.ShapeDtypeStruct((2 * ring, 2, width, rows), jnp.float32)
    field = pltpu.VMEM((layers, 2, 2, columns + window, rows), jnp.float32)
    total = pltpu.VMEM((2, 2, columns + window, rows), jnp.float32)
    wave_scratch = pltpu.VMEM(waves.shape, jnp.float32)
    dft_flops = count * 2 * 3 * 2 * window * (2 * window) ** 2

    def swap(value):
        return lax.ppermute(value, "probe", [(i, i ^ 1) for i in range(devices)])

    def route(step, band):
        pairs = []
        for r in range(regions):
            for d in range(devices):
                there = ((d // CORES + step) % ring) * CORES + d % CORES
                pairs.append((r * devices + d, ((r + band) % regions) * devices + there))
        return pairs

    def fetch(value, step, band):
        return lax.ppermute(value, ("region", "probe"), [(b, a) for a, b in route(step, band)])

    def give(value, step, band):
        return lax.ppermute(value, ("region", "probe"), route(step, band))

    steps = travel_order(ring)
    tile = jnp.swapaxes(object_slices, 2, 3)
    probe_t, intensity_t, direct, inverse, kernel = pl.pallas_call(
        prepare_kernel,
        out_shape=[
            jax.ShapeDtypeStruct(probe.shape, jnp.float32),
            jax.ShapeDtypeStruct(intensity.shape[1:], jnp.float32),
            jax.ShapeDtypeStruct(direct.shape, direct.dtype),
            jax.ShapeDtypeStruct(inverse.shape, inverse.dtype),
            jax.ShapeDtypeStruct(kernel.shape, kernel.dtype),
        ],
        in_specs=[HBM] * 5,
        out_specs=[VMEM] * 5,
        scratch_shapes=[
            pltpu.VMEM(probe.shape, jnp.float32),
            pltpu.VMEM(intensity.shape, jnp.float32),
            pltpu.SemaphoreType.DMA((5,)),
        ],
        compiler_params=PARAMS,
        cost_estimate=cost(dft_flops, 16 << 20),
    )(probe, intensity, direct, inverse, kernel)
    arrived = [tile] + [fetch(tile, *step) for step in steps[1:]]
    *arrived[1:], probe_t = lax.optimization_barrier((*arrived[1:], probe_t))
    gathered = []
    for value in arrived:
        gathered += [value, swap(value)]
    carried, keep_1, send_1 = pl.pallas_call(
        lambda *refs: main_kernel(ring, window, *refs),
        out_shape=[waves, units, units],
        in_specs=[SMEM] + [VMEM] * (5 + 4 * ring),
        out_specs=[VMEM] * 3,
        scratch_shapes=[field, wave_scratch, total],
        compiler_params=PARAMS,
        cost_estimate=cost(4 * dft_flops, 1 << 20),
    )(positions, probe_t, intensity_t, direct, inverse, kernel, *gathered)
    other_1 = swap(send_1)
    keep_0, send_0 = pl.pallas_call(
        lambda *refs: last_kernel(ring, window, *refs),
        out_shape=[units, units],
        in_specs=[SMEM] + [VMEM] * 5,
        out_specs=[VMEM] * 2,
        scratch_shapes=[total],
        compiler_params=PARAMS,
        cost_estimate=cost(2 * dft_flops, 1 << 20),
    )(positions, probe_t, carried, direct, inverse, kernel)
    other_1, send_0 = lax.optimization_barrier((other_1, send_0))
    other_0 = swap(send_0)
    both = pl.pallas_call(
        lambda *refs: pair_kernel(layers, *refs),
        out_shape=[unit] * len(steps),
        in_specs=[VMEM] * 4,
        out_specs=[VMEM] * len(steps),
        compiler_params=PARAMS,
    )(keep_0, other_0, keep_1, other_1)
    terms = [give(both[at], *steps[at]) for at in range(len(steps) - 1, 0, -1)] + [both[0]]
    gradient = pl.pallas_call(
        lambda *refs: sum_kernel(1.0 / (count * devices), *refs),
        out_shape=unit,
        in_specs=[VMEM] * len(steps),
        out_specs=VMEM,
        compiler_params=PARAMS,
    )(*terms)
    return jnp.swapaxes(gradient, 2, 3)


def solution(mesh):
    placed = (
        P("group", None, "region", "probe"),
        P("group", None, None),
        P("region", "probe", "group", None),
        P("region", "probe", "group"),
    )
    return jax.shard_map(
        body,
        mesh=mesh,
        in_specs=placed,
        out_specs=P("group", None, "region", "probe"),
        check_vma=False,
    )
```

```python
import math

import jax
import jax.numpy as jnp
import ml_dtypes
import numpy as np
from jax import lax
from jax.experimental import pallas as pl
from jax.experimental.pallas import tpu as pltpu
from jax.sharding import PartitionSpec as P

CORES = 2
PAIRED = 2
HALF = 64


def split_table(table):
    high = table.astype(ml_dtypes.bfloat16)
    low = (table - high.astype(np.float64)).astype(ml_dtypes.bfloat16)
    return np.stack([high, low])


def tables(window):
    indices = np.arange(window)
    angles = 2.0 * math.pi * ((indices[:, None] * indices[None, :]) % window) / window
    real, imag = np.cos(angles) / math.sqrt(window), -np.sin(angles) / math.sqrt(window)
    direct = np.block([[real, imag], [-imag, real]])
    inverse = np.block([[real, -imag], [imag, real]])
    frequency = np.where(indices < window // 2, indices, indices - window) / window
    phases = -60.0 * (frequency[:, None] ** 2 + frequency[None, :] ** 2)
    kernel = np.stack([np.cos(phases), np.sin(phases)]).astype(np.float32)
    return split_table(direct), split_table(inverse), kernel


def split(values):
    high = values.astype(jnp.bfloat16)
    low = (values - high.astype(jnp.float32)).astype(jnp.bfloat16)
    return high, low


def times_right(values, table_ref):
    high, low = split(values)
    rows = values.shape[0]
    both = jnp.dot(jnp.concatenate([high, low], axis=0), table_ref[0], preferred_element_type=jnp.float32)
    return both[:rows] + both[rows:] + jnp.dot(high, table_ref[1], preferred_element_type=jnp.float32)


def times_left(table_ref, values):
    high, low = split(values)
    table = jnp.concatenate([table_ref[0], table_ref[0], table_ref[1]], axis=1)
    stacked = jnp.concatenate([high, low, high], axis=0)
    return jnp.dot(table, stacked, preferred_element_type=jnp.float32)


def to_rows(values, window):
    count = values.shape[0] // window
    return jnp.concatenate(
        [
            jnp.concatenate(
                [values[n * window : (n + 1) * window, c * window : (c + 1) * window] for n in range(count)],
                axis=1,
            )
            for c in range(2)
        ],
        axis=0,
    )


def lanes(pairs):
    return jnp.concatenate([jnp.concatenate([re, im], axis=1) for re, im in pairs], axis=0)


def transform(pairs, right_ref, left_ref, window):
    halves = [times_right(jnp.concatenate(pair, axis=1), right_ref) for pair in pairs]
    out = []
    for at in range(0, len(pairs), PAIRED):
        group = halves[at : at + PAIRED]
        rows = [jnp.concatenate([half[:, c * window : (c + 1) * window] for half in group], axis=1) for c in range(2)]
        whole = times_left(left_ref, jnp.concatenate(rows, axis=0))
        for n in range(len(group)):
            columns = slice(n * window, (n + 1) * window)
            out.append((whole[:window, columns], whole[window:, columns]))
    return out


def fresnel(pairs, direct_ref, inverse_ref, kernel_ref, sign, window):
    k_re, k_im = kernel_ref[0], kernel_ref[1]
    if sign < 0:
        k_im = -k_im
    moved = [
        (k_re * re - k_im * im, k_re * im + k_im * re)
        for re, im in transform(pairs, direct_ref, inverse_ref, window)
    ]
    return transform(moved, inverse_ref, direct_ref, window)


def travel_order(ring):
    return [(0, 0)] + [(step, band) for band in range(2) for step in range(ring - 1, -1, -1) if step or band]


def assemble(unit_refs, field_ref, ring, window):
    me = lax.axis_index("probe")
    x, core = me // CORES, me % CORES
    layers = field_ref.shape[0]
    columns = field_ref.shape[3] - window
    at = 0
    for step, band in travel_order(ring):
        tile = lax.rem(x + step, ring)
        for owner in (core, 1 - core):
            where = pl.ds(pl.multiple_of((tile * CORES + owner) * HALF, HALF), HALF)
            for layer in range(layers):
                for c in range(2):
                    field_ref[layer, c, band, where, :] = unit_refs[at][layer, c]
            at += 1
    field_ref[:, :, :, columns:, :] = field_ref[:, :, :, :window, :]


def cut(field_ref, layer, position_ref, n, window):
    row, column = position_ref[0, n, 0], position_ref[0, n, 1]
    back = lax.rem(window - row, window)
    lane = lax.broadcasted_iota(jnp.int32, (window, window), 1)
    halves = []
    for c in range(2):
        first = pltpu.roll(field_ref[layer, c, 0, pl.ds(column, window), :], back, 1)
        second = pltpu.roll(field_ref[layer, c, 1, pl.ds(column, window), :], back, 1)
        halves.append(jnp.where(lane < window - row, first, second))
    return tuple(halves)


def deposit(total_ref, position_ref, n, pair, window):
    row, column = position_ref[0, n, 0], position_ref[0, n, 1]
    lane = lax.broadcasted_iota(jnp.int32, (window, window), 1)
    where = pl.ds(column, window)
    for c in range(2):
        turned = pltpu.roll(pair[c], row, 1)
        total_ref[c, 0, where, :] += jnp.where(lane >= row, turned, 0.0)
        total_ref[c, 1, where, :] += jnp.where(lane < row, turned, 0.0)


def hand_out(total_ref, keep_ref, send_ref, ring, window):
    me = lax.axis_index("probe")
    x, core = me // CORES, me % CORES
    columns = total_ref.shape[2] - window
    total_ref[:, :, :window, :] += total_ref[:, :, columns:, :]
    for at, (step, band) in enumerate(travel_order(ring)):
        tile = lax.rem(x + step, ring)
        for owner, ref in ((core, keep_ref), (1 - core, send_ref)):
            where = pl.ds(pl.multiple_of((tile * CORES + owner) * HALF, HALF), HALF)
            for c in range(2):
                ref[at, c] = total_ref[c, band, where, :]


def prepare_kernel(*refs):
    sources, outputs = refs[:5], refs[5:10]
    probe_ref, intensity_ref, sems = refs[10:]
    targets = (probe_ref, intensity_ref) + outputs[2:]
    copies = [pltpu.make_async_copy(a, b, sems.at[i]) for i, (a, b) in enumerate(zip(sources, targets))]
    for copy in copies:
        copy.start()
    copies[0].wait()
    for c in range(2):
        outputs[0][c] = probe_ref[c].T
    copies[1].wait()
    for n in range(intensity_ref.shape[1]):
        outputs[1][n] = intensity_ref[0, n].T
    for copy in copies[2:]:
        copy.wait()


def main_kernel(ring, window, position_ref, probe_ref, intensity_ref, direct_ref, inverse_ref, kernel_ref, *rest):
    unit_refs, (carried_ref, keep_ref, send_ref, field_ref, wave_ref, total_ref) = rest[:-6], rest[-6:]
    count = position_ref.shape[1]
    assemble(unit_refs, field_ref, ring, window)
    total_ref[...] = jnp.zeros_like(total_ref)
    probe_re, probe_im = probe_ref[0], probe_ref[1]
    exits = []
    for n in range(count):
        re, im = cut(field_ref, 0, position_ref, n, window)
        exits.append((probe_re * re - probe_im * im, probe_re * im + probe_im * re))
    waves = fresnel(exits, direct_ref, inverse_ref, kernel_ref, 1, window)
    exits = []
    for n in range(count):
        re, im = cut(field_ref, 1, position_ref, n, window)
        w_re, w_im = waves[n]
        wave_ref[n, 0] = w_re
        wave_ref[n, 1] = w_im
        exits.append((w_re * re - w_im * im, w_re * im + w_im * re))
    scaled = []
    for n, (re, im) in enumerate(transform(exits, direct_ref, inverse_ref, window)):
        misfit = re * re + im * im - intensity_ref[n]
        scaled.append((misfit * re, misfit * im))
    for n, (b_re, b_im) in enumerate(transform(scaled, inverse_ref, direct_ref, window)):
        w_re, w_im = wave_ref[n, 0], wave_ref[n, 1]
        p_re, p_im = cut(field_ref, 1, position_ref, n, window)
        carried_ref[n, 0] = p_re * b_re + p_im * b_im
        carried_ref[n, 1] = p_re * b_im - p_im * b_re
        gradient = (w_re * b_re + w_im * b_im, w_re * b_im - w_im * b_re)
        deposit(total_ref, position_ref, n, gradient, window)
    hand_out(total_ref, keep_ref, send_ref, ring, window)


def last_kernel(
    ring, window, position_ref, probe_ref, carried_ref, direct_ref, inverse_ref, kernel_ref, keep_ref, send_ref, total_ref
):
    count = position_ref.shape[1]
    total_ref[...] = jnp.zeros_like(total_ref)
    carried = [(carried_ref[n, 0], carried_ref[n, 1]) for n in range(count)]
    backs = fresnel(carried, direct_ref, inverse_ref, kernel_ref, -1, window)
    probe_re, probe_im = probe_ref[0], probe_ref[1]
    for n, (b_re, b_im) in enumerate(backs):
        gradient = (probe_re * b_re + probe_im * b_im, probe_re * b_im - probe_im * b_re)
        deposit(total_ref, position_ref, n, gradient, window)
    hand_out(total_ref, keep_ref, send_ref, ring, window)


def pair_kernel(layers, *refs):
    inputs, outputs = refs[: 2 * layers], refs[2 * layers :]
    for layer in range(layers):
        for at, out_ref in enumerate(outputs):
            out_ref[layer] = inputs[2 * layer][at] + inputs[2 * layer + 1][at]


def sum_kernel(scale, *refs):
    total = refs[0][...]
    for ref in refs[1:-1]:
        total += ref[...]
    refs[-1][...] = total * scale


VMEM = pl.BlockSpec(memory_space=pltpu.VMEM)
HBM = pl.BlockSpec(memory_space=pltpu.HBM)
SMEM = pl.BlockSpec(memory_space=pltpu.SMEM)
PARAMS = pltpu.CompilerParams(vmem_limit_bytes=40 << 20)


def cost(flops, moved):
    return pl.CostEstimate(flops=flops, bytes_accessed=moved, transcendentals=0)


def body(object_slices, probe, intensity, positions):
    layers, _, rows, width = object_slices.shape
    window = probe.shape[1]
    count = positions.shape[1]
    regions = lax.axis_size("region")
    devices = lax.axis_size("probe")
    ring = devices // CORES
    columns = devices * width
    direct, inverse, kernel = (jnp.asarray(t) for t in tables(window))
    unit = jax.ShapeDtypeStruct((layers, 2, width, rows), jnp.float32)
    waves = jax.ShapeDtypeStruct((count, 2, window, window), jnp.float32)
    units = jax.ShapeDtypeStruct((2 * ring, 2, width, rows), jnp.float32)
    field = pltpu.VMEM((layers, 2, 2, columns + window, rows), jnp.float32)
    total = pltpu.VMEM((2, 2, columns + window, rows), jnp.float32)
    wave_scratch = pltpu.VMEM(waves.shape, jnp.float32)
    dft_flops = count * 2 * 3 * 2 * window * (2 * window) ** 2

    def swap(value):
        return lax.ppermute(value, "probe", [(i, i ^ 1) for i in range(devices)])

    def route(step, band):
        pairs = []
        for r in range(regions):
            for d in range(devices):
                there = ((d // CORES + step) % ring) * CORES + d % CORES
                pairs.append((r * devices + d, ((r + band) % regions) * devices + there))
        return pairs

    def fetch(value, step, band):
        return lax.ppermute(value, ("region", "probe"), [(b, a) for a, b in route(step, band)])

    def give(value, step, band):
        return lax.ppermute(value, ("region", "probe"), route(step, band))

    steps = travel_order(ring)
    tile = jnp.swapaxes(object_slices, 2, 3)
    probe_t, intensity_t, direct, inverse, kernel = pl.pallas_call(
        prepare_kernel,
        out_shape=[
            jax.ShapeDtypeStruct(probe.shape, jnp.float32),
            jax.ShapeDtypeStruct(intensity.shape[1:], jnp.float32),
            jax.ShapeDtypeStruct(direct.shape, direct.dtype),
            jax.ShapeDtypeStruct(inverse.shape, inverse.dtype),
            jax.ShapeDtypeStruct(kernel.shape, kernel.dtype),
        ],
        in_specs=[HBM] * 5,
        out_specs=[VMEM] * 5,
        scratch_shapes=[
            pltpu.VMEM(probe.shape, jnp.float32),
            pltpu.VMEM(intensity.shape, jnp.float32),
            pltpu.SemaphoreType.DMA((5,)),
        ],
        compiler_params=PARAMS,
        cost_estimate=cost(dft_flops, 16 << 20),
    )(probe, intensity, direct, inverse, kernel)
    arrived = [tile] + [fetch(tile, *step) for step in steps[1:]]
    *arrived[1:], probe_t = lax.optimization_barrier((*arrived[1:], probe_t))
    gathered = []
    for value in arrived:
        gathered += [value, swap(value)]
    carried, keep_1, send_1 = pl.pallas_call(
        lambda *refs: main_kernel(ring, window, *refs),
        out_shape=[waves, units, units],
        in_specs=[SMEM] + [VMEM] * (5 + 4 * ring),
        out_specs=[VMEM] * 3,
        scratch_shapes=[field, wave_scratch, total],
        compiler_params=PARAMS,
        cost_estimate=cost(4 * dft_flops, 1 << 20),
    )(positions, probe_t, intensity_t, direct, inverse, kernel, *gathered)
    other_1 = swap(send_1)
    keep_0, send_0 = pl.pallas_call(
        lambda *refs: last_kernel(ring, window, *refs),
        out_shape=[units, units],
        in_specs=[SMEM] + [VMEM] * 5,
        out_specs=[VMEM] * 2,
        scratch_shapes=[total],
        compiler_params=PARAMS,
        cost_estimate=cost(2 * dft_flops, 1 << 20),
    )(positions, probe_t, carried, direct, inverse, kernel)
    other_1, send_0 = lax.optimization_barrier((other_1, send_0))
    other_0 = swap(send_0)
    both = pl.pallas_call(
        lambda *refs: pair_kernel(layers, *refs),
        out_shape=[unit] * len(steps),
        in_specs=[VMEM] * 4,
        out_specs=[VMEM] * len(steps),
        compiler_params=PARAMS,
    )(keep_0, other_0, keep_1, other_1)
    terms = [give(both[at], *steps[at]) for at in range(len(steps) - 1, 0, -1)] + [both[0]]
    gradient = pl.pallas_call(
        lambda *refs: sum_kernel(1.0 / (count * devices), *refs),
        out_shape=unit,
        in_specs=[VMEM] * len(steps),
        out_specs=VMEM,
        compiler_params=PARAMS,
    )(*terms)
    return jnp.swapaxes(gradient, 2, 3)


def solution(mesh):
    placed = (
        P("group", None, "region", "probe"),
        P("group", None, None),
        P("region", "probe", "group", None),
        P("region", "probe", "group"),
    )
    return jax.shard_map(
        body,
        mesh=mesh,
        in_specs=placed,
        out_specs=P("group", None, "region", "probe"),
        check_vma=False,
    )
```

```python
import math

import jax
import jax.numpy as jnp
import ml_dtypes
import numpy as np
from jax import lax
from jax.experimental import pallas as pl
from jax.experimental.pallas import tpu as pltpu
from jax.sharding import PartitionSpec as P

CORES = 2
PAIRED = 2
HALF = 64


def split_table(table):
    high = table.astype(ml_dtypes.bfloat16)
    low = (table - high.astype(np.float64)).astype(ml_dtypes.bfloat16)
    return np.stack([high, low])


def tables(window):
    indices = np.arange(window)
    angles = 2.0 * math.pi * ((indices[:, None] * indices[None, :]) % window) / window
    real, imag = np.cos(angles) / math.sqrt(window), -np.sin(angles) / math.sqrt(window)
    direct = np.block([[real, imag], [-imag, real]])
    inverse = np.block([[real, -imag], [imag, real]])
    frequency = np.where(indices < window // 2, indices, indices - window) / window
    phases = -60.0 * (frequency[:, None] ** 2 + frequency[None, :] ** 2)
    kernel = np.stack([np.cos(phases), np.sin(phases)]).astype(np.float32)
    return split_table(direct), split_table(inverse), kernel


def split(values):
    high = values.astype(jnp.bfloat16)
    low = (values - high.astype(jnp.float32)).astype(jnp.bfloat16)
    return high, low


def times_right(values, table_ref):
    high, low = split(values)
    rows = values.shape[0]
    both = jnp.dot(jnp.concatenate([high, low], axis=0), table_ref[0], preferred_element_type=jnp.float32)
    return both[:rows] + both[rows:] + jnp.dot(high, table_ref[1], preferred_element_type=jnp.float32)


def times_left(table_ref, values):
    high, low = split(values)
    table = jnp.concatenate([table_ref[0], table_ref[0], table_ref[1]], axis=1)
    stacked = jnp.concatenate([high, low, high], axis=0)
    return jnp.dot(table, stacked, preferred_element_type=jnp.float32)


def to_rows(values, window):
    count = values.shape[0] // window
    return jnp.concatenate(
        [
            jnp.concatenate(
                [values[n * window : (n + 1) * window, c * window : (c + 1) * window] for n in range(count)],
                axis=1,
            )
            for c in range(2)
        ],
        axis=0,
    )


def lanes(pairs):
    return jnp.concatenate([jnp.concatenate([re, im], axis=1) for re, im in pairs], axis=0)


def transform(pairs, right_ref, left_ref, window):
    halves = [times_right(jnp.concatenate(pair, axis=1), right_ref) for pair in pairs]
    out = []
    for at in range(0, len(pairs), PAIRED):
        group = halves[at : at + PAIRED]
        rows = [jnp.concatenate([half[:, c * window : (c + 1) * window] for half in group], axis=1) for c in range(2)]
        whole = times_left(left_ref, jnp.concatenate(rows, axis=0))
        for n in range(len(group)):
            columns = slice(n * window, (n + 1) * window)
            out.append((whole[:window, columns], whole[window:, columns]))
    return out


def fresnel(pairs, direct_ref, inverse_ref, kernel_ref, sign, window):
    k_re, k_im = kernel_ref[0], kernel_ref[1]
    if sign < 0:
        k_im = -k_im
    moved = [
        (k_re * re - k_im * im, k_re * im + k_im * re)
        for re, im in transform(pairs, direct_ref, inverse_ref, window)
    ]
    return transform(moved, inverse_ref, direct_ref, window)


def travel_order(ring):
    return [(0, 0), (0, 1)] + [(step, band) for band in range(2) for step in range(1, ring)]


def assemble(unit_refs, field_ref, ring, window):
    me = lax.axis_index("probe")
    x, core = me // CORES, me % CORES
    layers = field_ref.shape[0]
    columns = field_ref.shape[3] - window
    at = 0
    for step, band in travel_order(ring):
        tile = lax.rem(x + step, ring)
        for owner in (core, 1 - core):
            where = pl.ds(pl.multiple_of((tile * CORES + owner) * HALF, HALF), HALF)
            for layer in range(layers):
                for c in range(2):
                    field_ref[layer, c, band, where, :] = unit_refs[at][layer, c]
            at += 1
    field_ref[:, :, :, columns:, :] = field_ref[:, :, :, :window, :]


def cut(field_ref, layer, position_ref, n, window):
    row, column = position_ref[0, n, 0], position_ref[0, n, 1]
    back = lax.rem(window - row, window)
    lane = lax.broadcasted_iota(jnp.int32, (window, window), 1)
    halves = []
    for c in range(2):
        first = pltpu.roll(field_ref[layer, c, 0, pl.ds(column, window), :], back, 1)
        second = pltpu.roll(field_ref[layer, c, 1, pl.ds(column, window), :], back, 1)
        halves.append(jnp.where(lane < window - row, first, second))
    return tuple(halves)


def deposit(total_ref, position_ref, n, pair, window):
    row, column = position_ref[0, n, 0], position_ref[0, n, 1]
    lane = lax.broadcasted_iota(jnp.int32, (window, window), 1)
    where = pl.ds(column, window)
    for c in range(2):
        turned = pltpu.roll(pair[c], row, 1)
        total_ref[c, 0, where, :] += jnp.where(lane >= row, turned, 0.0)
        total_ref[c, 1, where, :] += jnp.where(lane < row, turned, 0.0)


def hand_out(total_ref, layer, keep_refs, send_refs, ring, window):
    me = lax.axis_index("probe")
    x, core = me // CORES, me % CORES
    columns = total_ref.shape[2] - window
    total_ref[:, :, :window, :] += total_ref[:, :, columns:, :]
    for at, (step, band) in enumerate(travel_order(ring)):
        tile = lax.rem(x + step, ring)
        for owner, ref in ((core, keep_refs[at]), (1 - core, send_refs[at])):
            where = pl.ds(pl.multiple_of((tile * CORES + owner) * HALF, HALF), HALF)
            for c in range(2):
                ref[layer, c] = total_ref[c, band, where, :]


def prepare_kernel(*refs):
    sources, outputs = refs[:5], refs[5:10]
    probe_ref, intensity_ref, sems = refs[10:]
    targets = (probe_ref, intensity_ref) + outputs[2:]
    copies = [pltpu.make_async_copy(a, b, sems.at[i]) for i, (a, b) in enumerate(zip(sources, targets))]
    for copy in copies:
        copy.start()
    copies[0].wait()
    for c in range(2):
        outputs[0][c] = probe_ref[c].T
    copies[1].wait()
    for n in range(intensity_ref.shape[1]):
        outputs[1][n] = intensity_ref[0, n].T
    for copy in copies[2:]:
        copy.wait()


def main_kernel(ring, window, position_ref, probe_ref, intensity_ref, direct_ref, inverse_ref, kernel_ref, *rest):
    unit_refs, rest = rest[: 4 * ring], rest[4 * ring :]
    keep_refs, send_refs, (field_ref, wave_ref, total_ref, first_total_ref) = rest[: 2 * ring], rest[2 * ring : -4], rest[-4:]
    count = position_ref.shape[1]
    assemble(unit_refs, field_ref, ring, window)
    total_ref[...] = jnp.zeros_like(total_ref)
    first_total_ref[...] = jnp.zeros_like(first_total_ref)
    probe_re, probe_im = probe_ref[0], probe_ref[1]
    exits = []
    for n in range(count):
        re, im = cut(field_ref, 0, position_ref, n, window)
        exits.append((probe_re * re - probe_im * im, probe_re * im + probe_im * re))
    waves = fresnel(exits, direct_ref, inverse_ref, kernel_ref, 1, window)
    exits = []
    for n in range(count):
        re, im = cut(field_ref, 1, position_ref, n, window)
        w_re, w_im = waves[n]
        wave_ref[n, 0] = w_re
        wave_ref[n, 1] = w_im
        exits.append((w_re * re - w_im * im, w_re * im + w_im * re))
    scaled = []
    for n, (re, im) in enumerate(transform(exits, direct_ref, inverse_ref, window)):
        misfit = re * re + im * im - intensity_ref[n]
        scaled.append((misfit * re, misfit * im))
    carried, gradients = [], []
    for n, (b_re, b_im) in enumerate(transform(scaled, inverse_ref, direct_ref, window)):
        w_re, w_im = wave_ref[n, 0], wave_ref[n, 1]
        p_re, p_im = cut(field_ref, 1, position_ref, n, window)
        carried.append((p_re * b_re + p_im * b_im, p_re * b_im - p_im * b_re))
        deposit(total_ref, position_ref, n, (w_re * b_re + w_im * b_im, w_re * b_im - w_im * b_re), window)
    hand_out(total_ref, 1, keep_refs, send_refs, ring, window)
    for n, (b_re, b_im) in enumerate(fresnel(carried, direct_ref, inverse_ref, kernel_ref, -1, window)):
        gradient = (probe_re * b_re + probe_im * b_im, probe_re * b_im - probe_im * b_re)
        deposit(first_total_ref, position_ref, n, gradient, window)
    hand_out(first_total_ref, 0, keep_refs, send_refs, ring, window)


def sum_kernel(scale, *refs):
    total = refs[0][...]
    for ref in refs[1:-1]:
        total += ref[...]
    refs[-1][...] = total * scale


VMEM = pl.BlockSpec(memory_space=pltpu.VMEM)
HBM = pl.BlockSpec(memory_space=pltpu.HBM)
SMEM = pl.BlockSpec(memory_space=pltpu.SMEM)
PARAMS = pltpu.CompilerParams(vmem_limit_bytes=40 << 20)


def cost(flops, moved):
    return pl.CostEstimate(flops=flops, bytes_accessed=moved, transcendentals=0)


def body(object_slices, probe, intensity, positions):
    layers, _, rows, width = object_slices.shape
    window = probe.shape[1]
    count = positions.shape[1]
    regions = lax.axis_size("region")
    devices = lax.axis_size("probe")
    ring = devices // CORES
    columns = devices * width
    direct, inverse, kernel = (jnp.asarray(t) for t in tables(window))
    unit = jax.ShapeDtypeStruct((layers, 2, width, rows), jnp.float32)
    field = pltpu.VMEM((layers, 2, 2, columns + window, rows), jnp.float32)
    total = pltpu.VMEM((2, 2, columns + window, rows), jnp.float32)
    wave_scratch = pltpu.VMEM((count, 2, window, window), jnp.float32)
    dft_flops = count * 2 * 3 * 2 * window * (2 * window) ** 2

    def swap(value):
        return lax.ppermute(value, "probe", [(i, i ^ 1) for i in range(devices)])

    def route(step, band):
        pairs = []
        for r in range(regions):
            for d in range(devices):
                there = ((d // CORES + step) % ring) * CORES + d % CORES
                pairs.append((r * devices + d, ((r + band) % regions) * devices + there))
        return pairs

    def fetch(value, step, band):
        return lax.ppermute(value, ("region", "probe"), [(b, a) for a, b in route(step, band)])

    def give(value, step, band):
        return lax.ppermute(value, ("region", "probe"), route(step, band))

    steps = travel_order(ring)
    tile = jnp.swapaxes(object_slices, 2, 3)
    probe_t, intensity_t, direct, inverse, kernel = pl.pallas_call(
        prepare_kernel,
        out_shape=[
            jax.ShapeDtypeStruct(probe.shape, jnp.float32),
            jax.ShapeDtypeStruct(intensity.shape[1:], jnp.float32),
            jax.ShapeDtypeStruct(direct.shape, direct.dtype),
            jax.ShapeDtypeStruct(inverse.shape, inverse.dtype),
            jax.ShapeDtypeStruct(kernel.shape, kernel.dtype),
        ],
        in_specs=[HBM] * 5,
        out_specs=[VMEM] * 5,
        scratch_shapes=[
            pltpu.VMEM(probe.shape, jnp.float32),
            pltpu.VMEM(intensity.shape, jnp.float32),
            pltpu.SemaphoreType.DMA((5,)),
        ],
        compiler_params=PARAMS,
        cost_estimate=cost(1, 1),
    )(*(pltpu.with_memory_space_constraint(value, pltpu.HBM) for value in (probe, intensity, direct, inverse, kernel)))
    arrived = [tile] + [fetch(tile, *step) for step in steps[1:]]
    early = [at for at, step in enumerate(steps) if at and not all(step)]
    late = [at for at, step in enumerate(steps) if all(step)]
    *values, probe_t = lax.optimization_barrier((*(arrived[at] for at in early), probe_t))
    arrived = {0: tile, **dict(zip(early, values)), **{at: arrived[at] for at in late}}
    swapped = {at: swap(arrived[at]) for at in [0] + early}
    values = lax.optimization_barrier(([arrived[at] for at in late], [swapped[at] for at in early]))
    arrived.update(zip(late, values[0]))
    swapped.update(zip(early, values[1]))
    swapped.update({at: swap(arrived[at]) for at in late})
    gathered = [value for at in range(len(steps)) for value in (arrived[at], swapped[at])]
    outputs = pl.pallas_call(
        lambda *refs: main_kernel(ring, window, *refs),
        out_shape=[unit] * (2 * len(steps)),
        in_specs=[SMEM] + [VMEM] * (5 + 4 * ring),
        out_specs=[VMEM] * (2 * len(steps)),
        scratch_shapes=[field, wave_scratch, total, total],
        compiler_params=PARAMS,
        cost_estimate=cost(6 * dft_flops, 8 << 20),
    )(positions, probe_t, intensity_t, direct, inverse, kernel, *gathered)
    keep, send = outputs[: len(steps)], outputs[len(steps) :]
    order = late + early
    other = {at: swap(send[at]) for at in order}
    own, other[order[0]] = lax.optimization_barrier((send[0], other[order[0]]))
    terms = [give(keep[at] + other[at], *steps[at]) for at in order]
    other_own = swap(own)
    gradient = pl.pallas_call(
        lambda *refs: sum_kernel(1.0 / (count * devices), *refs),
        out_shape=unit,
        in_specs=[VMEM] * (len(steps) + 1),
        out_specs=VMEM,
        compiler_params=PARAMS,
    )(keep[0], other_own, *terms)
    return jnp.swapaxes(gradient, 2, 3)


def solution(mesh):
    placed = (
        P("group", None, "region", "probe"),
        P("group", None, None),
        P("region", "probe", "group", None),
        P("region", "probe", "group"),
    )
    return jax.shard_map(
        body,
        mesh=mesh,
        in_specs=placed,
        out_specs=P("group", None, "region", "probe"),
        check_vma=False,
    )
```

```python
import math

import jax
import jax.numpy as jnp
import ml_dtypes
import numpy as np
from jax import lax
from jax.experimental import pallas as pl
from jax.experimental.pallas import tpu as pltpu
from jax.sharding import PartitionSpec as P

CORES = 2
PAIRED = 2
HALF = 64


def split_table(table):
    high = table.astype(ml_dtypes.bfloat16)
    low = (table - high.astype(np.float64)).astype(ml_dtypes.bfloat16)
    return np.stack([high, low])


def as_real(table):
    return np.block([[table.real, table.imag], [-table.imag, table.real]])


def tables(window):
    indices = np.arange(window)
    angles = 2.0 * math.pi * ((indices[:, None] * indices[None, :]) % window) / window
    transform = np.exp(-1j * angles) / math.sqrt(window)
    frequency = np.where(indices < window // 2, indices, indices - window) / window
    step = (transform.conj() * np.exp(-60j * frequency**2)) @ transform
    step = (step + step.T) / 2
    return np.stack([split_table(as_real(m)) for m in (transform, transform.conj(), step, step.conj())])


def split(values):
    high = values.astype(jnp.bfloat16)
    low = (values - high.astype(jnp.float32)).astype(jnp.bfloat16)
    return high, low


def times_right(values, table_ref):
    high, low = split(values)
    rows = values.shape[0]
    both = jnp.dot(jnp.concatenate([high, low], axis=0), table_ref[0], preferred_element_type=jnp.float32)
    return both[:rows] + both[rows:] + jnp.dot(high, table_ref[1], preferred_element_type=jnp.float32)


def times_left(table_ref, values):
    high, low = split(values)
    table = jnp.concatenate([table_ref[0], table_ref[0], table_ref[1]], axis=1)
    stacked = jnp.concatenate([high, low, high], axis=0)
    return jnp.dot(table, stacked, preferred_element_type=jnp.float32)


def transform(pairs, right_ref, left_ref, window):
    halves = [times_right(jnp.concatenate(pair, axis=1), right_ref) for pair in pairs]
    out = []
    for at in range(0, len(pairs), PAIRED):
        group = halves[at : at + PAIRED]
        rows = [jnp.concatenate([half[:, c * window : (c + 1) * window] for half in group], axis=1) for c in range(2)]
        whole = times_left(left_ref, jnp.concatenate(rows, axis=0))
        for n in range(len(group)):
            columns = slice(n * window, (n + 1) * window)
            out.append((whole[:window, columns], whole[window:, columns]))
    return out


def travel_order(ring):
    return [(0, 0), (0, 1)] + [(step, band) for band in range(2) for step in range(1, ring)]


def assemble(unit_refs, field_ref, ring, window):
    me = lax.axis_index("probe")
    x, core = me // CORES, me % CORES
    layers = field_ref.shape[0]
    columns = field_ref.shape[3] - window
    at = 0
    for step, band in travel_order(ring):
        tile = lax.rem(x + step, ring)
        for owner in (core, 1 - core):
            where = pl.ds(pl.multiple_of((tile * CORES + owner) * HALF, HALF), HALF)
            for layer in range(layers):
                for c in range(2):
                    field_ref[layer, c, band, where, :] = unit_refs[at][layer, c]
            at += 1
    field_ref[:, :, :, columns:, :] = field_ref[:, :, :, :window, :]


def cut(field_ref, layer, position_ref, n, window):
    row, column = position_ref[0, n, 0], position_ref[0, n, 1]
    back = lax.rem(window - row, window)
    lane = lax.broadcasted_iota(jnp.int32, (window, window), 1)
    halves = []
    for c in range(2):
        first = pltpu.roll(field_ref[layer, c, 0, pl.ds(column, window), :], back, 1)
        second = pltpu.roll(field_ref[layer, c, 1, pl.ds(column, window), :], back, 1)
        halves.append(jnp.where(lane < window - row, first, second))
    return tuple(halves)


def deposit(total_ref, position_ref, n, pair, window):
    row, column = position_ref[0, n, 0], position_ref[0, n, 1]
    lane = lax.broadcasted_iota(jnp.int32, (window, window), 1)
    where = pl.ds(column, window)
    for c in range(2):
        turned = pltpu.roll(pair[c], row, 1)
        total_ref[c, 0, where, :] += jnp.where(lane >= row, turned, 0.0)
        total_ref[c, 1, where, :] += jnp.where(lane < row, turned, 0.0)


def hand_out(total_ref, layer, keep_refs, send_refs, ring, window):
    me = lax.axis_index("probe")
    x, core = me // CORES, me % CORES
    columns = total_ref.shape[2] - window
    total_ref[:, :, :window, :] += total_ref[:, :, columns:, :]
    for at, (step, band) in enumerate(travel_order(ring)):
        tile = lax.rem(x + step, ring)
        for owner, ref in ((core, keep_refs[at]), (1 - core, send_refs[at])):
            where = pl.ds(pl.multiple_of((tile * CORES + owner) * HALF, HALF), HALF)
            for c in range(2):
                ref[layer, c] = total_ref[c, band, where, :]


def prepare_kernel(*refs):
    sources, outputs = refs[:3], refs[3:6]
    probe_ref, intensity_ref, sems = refs[6:]
    targets = (probe_ref, intensity_ref) + outputs[2:]
    copies = [pltpu.make_async_copy(a, b, sems.at[i]) for i, (a, b) in enumerate(zip(sources, targets))]
    for copy in copies:
        copy.start()
    copies[0].wait()
    for c in range(2):
        outputs[0][c] = probe_ref[c].T
    copies[1].wait()
    for n in range(intensity_ref.shape[1]):
        outputs[1][n] = intensity_ref[0, n].T
    for copy in copies[2:]:
        copy.wait()


def main_kernel(ring, window, position_ref, probe_ref, intensity_ref, table_ref, *rest):
    direct_ref, inverse_ref, forth_ref, back_ref = (table_ref.at[i] for i in range(4))
    unit_refs, rest = rest[: 4 * ring], rest[4 * ring :]
    keep_refs, send_refs, (field_ref, wave_ref, total_ref, first_total_ref) = rest[: 2 * ring], rest[2 * ring : -4], rest[-4:]
    count = position_ref.shape[1]
    assemble(unit_refs, field_ref, ring, window)
    total_ref[...] = jnp.zeros_like(total_ref)
    first_total_ref[...] = jnp.zeros_like(first_total_ref)
    probe_re, probe_im = probe_ref[0], probe_ref[1]
    exits = []
    for n in range(count):
        re, im = cut(field_ref, 0, position_ref, n, window)
        exits.append((probe_re * re - probe_im * im, probe_re * im + probe_im * re))
    waves = transform(exits, forth_ref, back_ref, window)
    exits = []
    for n in range(count):
        re, im = cut(field_ref, 1, position_ref, n, window)
        w_re, w_im = waves[n]
        wave_ref[n, 0] = w_re
        wave_ref[n, 1] = w_im
        exits.append((w_re * re - w_im * im, w_re * im + w_im * re))
    scaled = []
    for n, (re, im) in enumerate(transform(exits, direct_ref, inverse_ref, window)):
        misfit = re * re + im * im - intensity_ref[n]
        scaled.append((misfit * re, misfit * im))
    carried, gradients = [], []
    for n, (b_re, b_im) in enumerate(transform(scaled, inverse_ref, direct_ref, window)):
        w_re, w_im = wave_ref[n, 0], wave_ref[n, 1]
        p_re, p_im = cut(field_ref, 1, position_ref, n, window)
        carried.append((p_re * b_re + p_im * b_im, p_re * b_im - p_im * b_re))
        deposit(total_ref, position_ref, n, (w_re * b_re + w_im * b_im, w_re * b_im - w_im * b_re), window)
    hand_out(total_ref, 1, keep_refs, send_refs, ring, window)
    for n, (b_re, b_im) in enumerate(transform(carried, back_ref, forth_ref, window)):
        gradient = (probe_re * b_re + probe_im * b_im, probe_re * b_im - probe_im * b_re)
        deposit(first_total_ref, position_ref, n, gradient, window)
    hand_out(first_total_ref, 0, keep_refs, send_refs, ring, window)


def sum_kernel(scale, *refs):
    total = refs[0][...]
    for ref in refs[1:-1]:
        total += ref[...]
    refs[-1][...] = total * scale


VMEM = pl.BlockSpec(memory_space=pltpu.VMEM)
HBM = pl.BlockSpec(memory_space=pltpu.HBM)
SMEM = pl.BlockSpec(memory_space=pltpu.SMEM)
PARAMS = pltpu.CompilerParams(vmem_limit_bytes=40 << 20)


def cost(flops, moved):
    return pl.CostEstimate(flops=flops, bytes_accessed=moved, transcendentals=0)


def body(object_slices, probe, intensity, positions):
    layers, _, rows, width = object_slices.shape
    window = probe.shape[1]
    count = positions.shape[1]
    regions = lax.axis_size("region")
    devices = lax.axis_size("probe")
    ring = devices // CORES
    columns = devices * width
    table = jnp.asarray(tables(window))
    unit = jax.ShapeDtypeStruct((layers, 2, width, rows), jnp.float32)
    field = pltpu.VMEM((layers, 2, 2, columns + window, rows), jnp.float32)
    total = pltpu.VMEM((2, 2, columns + window, rows), jnp.float32)
    wave_scratch = pltpu.VMEM((count, 2, window, window), jnp.float32)
    dft_flops = count * 2 * 3 * 2 * window * (2 * window) ** 2

    def swap(value):
        return lax.ppermute(value, "probe", [(i, i ^ 1) for i in range(devices)])

    def route(step, band):
        pairs = []
        for r in range(regions):
            for d in range(devices):
                there = ((d // CORES + step) % ring) * CORES + d % CORES
                pairs.append((r * devices + d, ((r + band) % regions) * devices + there))
        return pairs

    def fetch(value, step, band):
        return lax.ppermute(value, ("region", "probe"), [(b, a) for a, b in route(step, band)])

    def give(value, step, band):
        return lax.ppermute(value, ("region", "probe"), route(step, band))

    steps = travel_order(ring)
    tile = jnp.swapaxes(object_slices, 2, 3)
    probe_t, intensity_t, table = pl.pallas_call(
        prepare_kernel,
        out_shape=[
            jax.ShapeDtypeStruct(probe.shape, jnp.float32),
            jax.ShapeDtypeStruct(intensity.shape[1:], jnp.float32),
            jax.ShapeDtypeStruct(table.shape, table.dtype),
        ],
        in_specs=[HBM] * 3,
        out_specs=[VMEM] * 3,
        scratch_shapes=[
            pltpu.VMEM(probe.shape, jnp.float32),
            pltpu.VMEM(intensity.shape, jnp.float32),
            pltpu.SemaphoreType.DMA((3,)),
        ],
        compiler_params=PARAMS,
        cost_estimate=cost(1, 1),
    )(*(pltpu.with_memory_space_constraint(value, pltpu.HBM) for value in (probe, intensity, table)))
    arrived = [tile] + [fetch(tile, *step) for step in steps[1:]]
    early = [at for at, step in enumerate(steps) if at and not all(step)]
    late = [at for at, step in enumerate(steps) if all(step)]
    *values, probe_t = lax.optimization_barrier((*(arrived[at] for at in early), probe_t))
    arrived = {0: tile, **dict(zip(early, values)), **{at: arrived[at] for at in late}}
    swapped = {at: swap(arrived[at]) for at in [0] + early}
    values = lax.optimization_barrier(([arrived[at] for at in late], [swapped[at] for at in early]))
    arrived.update(zip(late, values[0]))
    swapped.update(zip(early, values[1]))
    swapped.update({at: swap(arrived[at]) for at in late})
    gathered = [value for at in range(len(steps)) for value in (arrived[at], swapped[at])]
    outputs = pl.pallas_call(
        lambda *refs: main_kernel(ring, window, *refs),
        out_shape=[unit] * (2 * len(steps)),
        in_specs=[SMEM] + [VMEM] * (3 + 4 * ring),
        out_specs=[VMEM] * (2 * len(steps)),
        scratch_shapes=[field, wave_scratch, total, total],
        compiler_params=PARAMS,
        cost_estimate=cost(4 * dft_flops, 8 << 20),
    )(positions, probe_t, intensity_t, table, *gathered)
    keep, send = outputs[: len(steps)], outputs[len(steps) :]
    order = late + early[::-1]
    other = {at: swap(send[at]) for at in order}
    own, other[order[0]] = lax.optimization_barrier((send[0], other[order[0]]))
    terms = [give(keep[at] + other[at], *steps[at]) for at in order]
    other_own = swap(own)
    gradient = pl.pallas_call(
        lambda *refs: sum_kernel(1.0 / (count * devices), *refs),
        out_shape=unit,
        in_specs=[VMEM] * (len(steps) + 1),
        out_specs=VMEM,
        compiler_params=PARAMS,
    )(keep[0], other_own, *terms)
    return jnp.swapaxes(gradient, 2, 3)


def solution(mesh):
    placed = (
        P("group", None, "region", "probe"),
        P("group", None, None),
        P("region", "probe", "group", None),
        P("region", "probe", "group"),
    )
    return jax.shard_map(
        body,
        mesh=mesh,
        in_specs=placed,
        out_specs=P("group", None, "region", "probe"),
        check_vma=False,
    )
```

```python
import math

import jax
import jax.numpy as jnp
import ml_dtypes
import numpy as np
from jax import lax
from jax.experimental import pallas as pl
from jax.experimental.pallas import tpu as pltpu
from jax.sharding import PartitionSpec as P

CORES = 2
PAIRED = 2
HALF = 64


def split_table(table):
    high = table.astype(ml_dtypes.bfloat16)
    low = (table - high.astype(np.float64)).astype(ml_dtypes.bfloat16)
    return np.stack([high, low])


def as_real(table):
    return np.block([[table.real, table.imag], [-table.imag, table.real]])


def tables(window):
    indices = np.arange(window)
    angles = 2.0 * math.pi * ((indices[:, None] * indices[None, :]) % window) / window
    transform = np.exp(-1j * angles) / math.sqrt(window)
    frequency = np.where(indices < window // 2, indices, indices - window) / window
    step = (transform.conj() * np.exp(-60j * frequency**2)) @ transform
    step = (step + step.T) / 2
    return np.stack([split_table(as_real(m)) for m in (transform, transform.conj(), step, step.conj())])


def split(values):
    high = values.astype(jnp.bfloat16)
    low = (values - high.astype(jnp.float32)).astype(jnp.bfloat16)
    return high, low


def times_right(values, table_ref):
    high, low = split(values)
    rows = values.shape[0]
    both = jnp.dot(jnp.concatenate([high, low], axis=0), table_ref[0], preferred_element_type=jnp.float32)
    return both[:rows] + both[rows:] + jnp.dot(high, table_ref[1], preferred_element_type=jnp.float32)


def times_left(table_ref, values):
    high, low = split(values)
    table = jnp.concatenate([table_ref[0], table_ref[0], table_ref[1]], axis=1)
    stacked = jnp.concatenate([high, low, high], axis=0)
    return jnp.dot(table, stacked, preferred_element_type=jnp.float32)


def transform(pairs, right_ref, left_ref, window):
    halves = []
    for at in range(0, len(pairs), PAIRED):
        group = pairs[at : at + PAIRED]
        rows = [jnp.concatenate([pair[c] for pair in group], axis=1) for c in range(2)]
        whole = times_left(left_ref, jnp.concatenate(rows, axis=0))
        for n in range(len(group)):
            columns = slice(n * window, (n + 1) * window)
            halves.append(jnp.concatenate([whole[:window, columns], whole[window:, columns]], axis=1))
    outs = [times_right(half, right_ref) for half in halves]
    return [(out[:, :window], out[:, window:]) for out in outs]


def travel_order(ring):
    return [(0, 0), (0, 1)] + [(step, band) for band in range(2) for step in range(1, ring)]


def assemble(unit_refs, field_ref, ring, window):
    me = lax.axis_index("probe")
    x, core = me // CORES, me % CORES
    layers = field_ref.shape[0]
    columns = field_ref.shape[3] - window
    at = 0
    for step, band in travel_order(ring):
        tile = lax.rem(x + step, ring)
        for owner in (core, 1 - core):
            where = pl.ds(pl.multiple_of((tile * CORES + owner) * HALF, HALF), HALF)
            for layer in range(layers):
                for c in range(2):
                    field_ref[layer, c, band, where, :] = unit_refs[at][layer, c]
            at += 1
    field_ref[:, :, :, columns:, :] = field_ref[:, :, :, :window, :]


def cut(field_ref, layer, position_ref, n, window):
    row, column = position_ref[0, n, 0], position_ref[0, n, 1]
    back = lax.rem(window - row, window)
    lane = lax.broadcasted_iota(jnp.int32, (window, window), 1)
    halves = []
    for c in range(2):
        first = pltpu.roll(field_ref[layer, c, 0, pl.ds(column, window), :], back, 1)
        second = pltpu.roll(field_ref[layer, c, 1, pl.ds(column, window), :], back, 1)
        halves.append(jnp.where(lane < window - row, first, second))
    return tuple(halves)


def deposit(total_ref, position_ref, n, pair, window):
    row, column = position_ref[0, n, 0], position_ref[0, n, 1]
    lane = lax.broadcasted_iota(jnp.int32, (window, window), 1)
    where = pl.ds(column, window)
    for c in range(2):
        turned = pltpu.roll(pair[c], row, 1)
        total_ref[c, 0, where, :] += jnp.where(lane >= row, turned, 0.0)
        total_ref[c, 1, where, :] += jnp.where(lane < row, turned, 0.0)


def hand_out(total_ref, layer, keep_refs, send_refs, ring, window):
    me = lax.axis_index("probe")
    x, core = me // CORES, me % CORES
    columns = total_ref.shape[2] - window
    total_ref[:, :, :window, :] += total_ref[:, :, columns:, :]
    for at, (step, band) in enumerate(travel_order(ring)):
        tile = lax.rem(x + step, ring)
        for owner, ref in ((core, keep_refs[at]), (1 - core, send_refs[at])):
            where = pl.ds(pl.multiple_of((tile * CORES + owner) * HALF, HALF), HALF)
            for c in range(2):
                ref[layer, c] = total_ref[c, band, where, :]


def prepare_kernel(*refs):
    sources, outputs = refs[:3], refs[3:6]
    probe_ref, intensity_ref, sems = refs[6:]
    targets = (probe_ref, intensity_ref) + outputs[2:]
    copies = [pltpu.make_async_copy(a, b, sems.at[i]) for i, (a, b) in enumerate(zip(sources, targets))]
    for copy in copies:
        copy.start()
    copies[0].wait()
    for c in range(2):
        outputs[0][c] = probe_ref[c].T
    copies[1].wait()
    for n in range(intensity_ref.shape[1]):
        outputs[1][n] = intensity_ref[0, n].T
    for copy in copies[2:]:
        copy.wait()


def main_kernel(ring, window, position_ref, probe_ref, intensity_ref, table_ref, *rest):
    direct_ref, inverse_ref, forth_ref, back_ref = (table_ref.at[i] for i in range(4))
    unit_refs, rest = rest[: 4 * ring], rest[4 * ring :]
    keep_refs, send_refs, (field_ref, wave_ref, total_ref, first_total_ref) = rest[: 2 * ring], rest[2 * ring : -4], rest[-4:]
    count = position_ref.shape[1]
    assemble(unit_refs, field_ref, ring, window)
    total_ref[...] = jnp.zeros_like(total_ref)
    first_total_ref[...] = jnp.zeros_like(first_total_ref)
    probe_re, probe_im = probe_ref[0], probe_ref[1]
    exits = []
    for n in range(count):
        re, im = cut(field_ref, 0, position_ref, n, window)
        exits.append((probe_re * re - probe_im * im, probe_re * im + probe_im * re))
    waves = transform(exits, forth_ref, back_ref, window)
    exits = []
    for n in range(count):
        re, im = cut(field_ref, 1, position_ref, n, window)
        w_re, w_im = waves[n]
        wave_ref[n, 0] = w_re
        wave_ref[n, 1] = w_im
        exits.append((w_re * re - w_im * im, w_re * im + w_im * re))
    scaled = []
    for n, (re, im) in enumerate(transform(exits, direct_ref, inverse_ref, window)):
        misfit = re * re + im * im - intensity_ref[n]
        scaled.append((misfit * re, misfit * im))
    carried, gradients = [], []
    for n, (b_re, b_im) in enumerate(transform(scaled, inverse_ref, direct_ref, window)):
        w_re, w_im = wave_ref[n, 0], wave_ref[n, 1]
        p_re, p_im = cut(field_ref, 1, position_ref, n, window)
        carried.append((p_re * b_re + p_im * b_im, p_re * b_im - p_im * b_re))
        deposit(total_ref, position_ref, n, (w_re * b_re + w_im * b_im, w_re * b_im - w_im * b_re), window)
    hand_out(total_ref, 1, keep_refs, send_refs, ring, window)
    for n, (b_re, b_im) in enumerate(transform(carried, back_ref, forth_ref, window)):
        gradient = (probe_re * b_re + probe_im * b_im, probe_re * b_im - probe_im * b_re)
        deposit(first_total_ref, position_ref, n, gradient, window)
    hand_out(first_total_ref, 0, keep_refs, send_refs, ring, window)


def sum_kernel(scale, *refs):
    total = refs[0][...]
    for ref in refs[1:-1]:
        total += ref[...]
    refs[-1][...] = total * scale


VMEM = pl.BlockSpec(memory_space=pltpu.VMEM)
HBM = pl.BlockSpec(memory_space=pltpu.HBM)
SMEM = pl.BlockSpec(memory_space=pltpu.SMEM)
PARAMS = pltpu.CompilerParams(vmem_limit_bytes=40 << 20)


def cost(flops, moved):
    return pl.CostEstimate(flops=flops, bytes_accessed=moved, transcendentals=0)


def body(object_slices, probe, intensity, positions):
    layers, _, rows, width = object_slices.shape
    window = probe.shape[1]
    count = positions.shape[1]
    regions = lax.axis_size("region")
    devices = lax.axis_size("probe")
    ring = devices // CORES
    columns = devices * width
    table = jnp.asarray(tables(window))
    unit = jax.ShapeDtypeStruct((layers, 2, width, rows), jnp.float32)
    field = pltpu.VMEM((layers, 2, 2, columns + window, rows), jnp.float32)
    total = pltpu.VMEM((2, 2, columns + window, rows), jnp.float32)
    wave_scratch = pltpu.VMEM((count, 2, window, window), jnp.float32)
    dft_flops = count * 2 * 3 * 2 * window * (2 * window) ** 2

    def swap(value):
        return lax.ppermute(value, "probe", [(i, i ^ 1) for i in range(devices)])

    def route(step, band):
        pairs = []
        for r in range(regions):
            for d in range(devices):
                there = ((d // CORES + step) % ring) * CORES + d % CORES
                pairs.append((r * devices + d, ((r + band) % regions) * devices + there))
        return pairs

    def fetch(value, step, band):
        return lax.ppermute(value, ("region", "probe"), [(b, a) for a, b in route(step, band)])

    def give(value, step, band):
        return lax.ppermute(value, ("region", "probe"), route(step, band))

    steps = travel_order(ring)
    tile = jnp.swapaxes(object_slices, 2, 3)
    probe_t, intensity_t, table = pl.pallas_call(
        prepare_kernel,
        out_shape=[
            jax.ShapeDtypeStruct(probe.shape, jnp.float32),
            jax.ShapeDtypeStruct(intensity.shape[1:], jnp.float32),
            jax.ShapeDtypeStruct(table.shape, table.dtype),
        ],
        in_specs=[HBM] * 3,
        out_specs=[VMEM] * 3,
        scratch_shapes=[
            pltpu.VMEM(probe.shape, jnp.float32),
            pltpu.VMEM(intensity.shape, jnp.float32),
            pltpu.SemaphoreType.DMA((3,)),
        ],
        compiler_params=PARAMS,
        cost_estimate=cost(1, 1),
    )(*(pltpu.with_memory_space_constraint(value, pltpu.HBM) for value in (probe, intensity, table)))
    early = [at for at, step in enumerate(steps) if all(step)]
    late = [at for at, step in enumerate(steps) if at and not all(step)]
    arrived = {at: fetch(tile, *steps[at]) for at in early + late}
    values, probe_t = lax.optimization_barrier(([arrived[at] for at in early], probe_t))
    arrived[0] = tile
    arrived.update(zip(early, values))
    swapped = {at: swap(arrived[at]) for at in [0] + early}
    values = lax.optimization_barrier(([arrived[at] for at in late], [swapped[at] for at in early]))
    arrived.update(zip(late, values[0]))
    swapped.update(zip(early, values[1]))
    swapped.update({at: swap(arrived[at]) for at in late})
    gathered = [value for at in range(len(steps)) for value in (arrived[at], swapped[at])]
    outputs = pl.pallas_call(
        lambda *refs: main_kernel(ring, window, *refs),
        out_shape=[unit] * (2 * len(steps)),
        in_specs=[SMEM] + [VMEM] * (3 + 4 * ring),
        out_specs=[VMEM] * (2 * len(steps)),
        scratch_shapes=[field, wave_scratch, total, total],
        compiler_params=PARAMS,
        cost_estimate=cost(4 * dft_flops, 8 << 20),
    )(positions, probe_t, intensity_t, table, *gathered)
    keep, send = outputs[: len(steps)], outputs[len(steps) :]
    order = early + late
    other = {at: swap(send[at]) for at in order}
    own, other[order[0]] = lax.optimization_barrier((send[0], other[order[0]]))
    terms = [give(keep[at] + other[at], *steps[at]) for at in order]
    other_own = swap(own)
    gradient = pl.pallas_call(
        lambda *refs: sum_kernel(1.0 / (count * devices), *refs),
        out_shape=unit,
        in_specs=[VMEM] * (len(steps) + 1),
        out_specs=VMEM,
        compiler_params=PARAMS,
    )(keep[0], other_own, *terms)
    return jnp.swapaxes(gradient, 2, 3)


def solution(mesh):
    placed = (
        P("group", None, "region", "probe"),
        P("group", None, None),
        P("region", "probe", "group", None),
        P("region", "probe", "group"),
    )
    return jax.shard_map(
        body,
        mesh=mesh,
        in_specs=placed,
        out_specs=P("group", None, "region", "probe"),
        check_vma=False,
    )
```

```python
import math

import jax
import jax.numpy as jnp
import ml_dtypes
import numpy as np
from jax import lax
from jax.experimental import pallas as pl
from jax.experimental.pallas import tpu as pltpu
from jax.sharding import PartitionSpec as P

CORES = 2
PAIRED = 2
HALF = 64


def split_table(table):
    high = table.astype(ml_dtypes.bfloat16)
    low = (table - high.astype(np.float64)).astype(ml_dtypes.bfloat16)
    return np.stack([high, low])


def as_real(table):
    return np.block([[table.real, table.imag], [-table.imag, table.real]])


def tables(window):
    indices = np.arange(window)
    angles = 2.0 * math.pi * ((indices[:, None] * indices[None, :]) % window) / window
    transform = np.exp(-1j * angles) / math.sqrt(window)
    frequency = np.where(indices < window // 2, indices, indices - window) / window
    step = (transform.conj() * np.exp(-60j * frequency**2)) @ transform
    step = (step + step.T) / 2
    return np.stack([split_table(as_real(m)) for m in (transform, transform.conj(), step, step.conj())])


def split(values):
    high = values.astype(jnp.bfloat16)
    low = (values - high.astype(jnp.float32)).astype(jnp.bfloat16)
    return high, low


def times_right(values, table_ref):
    high, low = split(values)
    rows = values.shape[0]
    both = jnp.dot(jnp.concatenate([high, low], axis=0), table_ref[0], preferred_element_type=jnp.float32)
    return both[:rows] + both[rows:] + jnp.dot(high, table_ref[1], preferred_element_type=jnp.float32)


def times_left(table_ref, values):
    high, low = split(values)
    table = jnp.concatenate([table_ref[0], table_ref[0], table_ref[1]], axis=1)
    stacked = jnp.concatenate([high, low, high], axis=0)
    return jnp.dot(table, stacked, preferred_element_type=jnp.float32)


def transform(pairs, right_ref, left_ref, window):
    halves = []
    for at in range(0, len(pairs), PAIRED):
        group = pairs[at : at + PAIRED]
        rows = [jnp.concatenate([pair[c] for pair in group], axis=1) for c in range(2)]
        whole = times_left(left_ref, jnp.concatenate(rows, axis=0))
        for n in range(len(group)):
            columns = slice(n * window, (n + 1) * window)
            halves.append(jnp.concatenate([whole[:window, columns], whole[window:, columns]], axis=1))
    outs = [times_right(half, right_ref) for half in halves]
    return [(out[:, :window], out[:, window:]) for out in outs]


def travel_order(ring):
    return [(0, 0), (0, 1)] + [(step, band) for band in range(2) for step in range(1, ring)]


def assemble(unit_refs, field_ref, ring, window):
    me = lax.axis_index("probe")
    x, core = me // CORES, me % CORES
    layers = field_ref.shape[0]
    columns = field_ref.shape[3] - window
    at = 0
    for step, band in travel_order(ring):
        tile = lax.rem(x + step, ring)
        for owner in (core, 1 - core):
            where = pl.ds(pl.multiple_of((tile * CORES + owner) * HALF, HALF), HALF)
            for layer in range(layers):
                for c in range(2):
                    field_ref[layer, c, band, where, :] = unit_refs[at][layer, c]
            at += 1
    field_ref[:, :, :, columns:, :] = field_ref[:, :, :, :window, :]


def cut(field_ref, layer, position_ref, n, window):
    row, column = position_ref[0, n, 0], position_ref[0, n, 1]
    back = lax.rem(window - row, window)
    lane = lax.broadcasted_iota(jnp.int32, (window, window), 1)
    halves = []
    for c in range(2):
        first = pltpu.roll(field_ref[layer, c, 0, pl.ds(column, window), :], back, 1)
        second = pltpu.roll(field_ref[layer, c, 1, pl.ds(column, window), :], back, 1)
        halves.append(jnp.where(lane < window - row, first, second))
    return tuple(halves)


def deposit(total_ref, position_ref, n, pair, window):
    row, column = position_ref[0, n, 0], position_ref[0, n, 1]
    lane = lax.broadcasted_iota(jnp.int32, (window, window), 1)
    where = pl.ds(column, window)
    for c in range(2):
        turned = pltpu.roll(pair[c], row, 1)
        total_ref[c, 0, where, :] += jnp.where(lane >= row, turned, 0.0)
        total_ref[c, 1, where, :] += jnp.where(lane < row, turned, 0.0)


def hand_out(total_ref, layer, keep_refs, send_refs, ring, window):
    me = lax.axis_index("probe")
    x, core = me // CORES, me % CORES
    columns = total_ref.shape[2] - window
    total_ref[:, :, :window, :] += total_ref[:, :, columns:, :]
    for at, (step, band) in enumerate(travel_order(ring)):
        tile = lax.rem(x + step, ring)
        for owner, ref in ((core, keep_refs[at]), (1 - core, send_refs[at])):
            where = pl.ds(pl.multiple_of((tile * CORES + owner) * HALF, HALF), HALF)
            for c in range(2):
                ref[layer, c] = total_ref[c, band, where, :]


def prepare_kernel(*refs):
    sources, outputs = refs[:3], refs[3:6]
    probe_ref, intensity_ref, sems = refs[6:]
    targets = (probe_ref, intensity_ref) + outputs[2:]
    copies = [pltpu.make_async_copy(a, b, sems.at[i]) for i, (a, b) in enumerate(zip(sources, targets))]
    for copy in copies:
        copy.start()
    copies[0].wait()
    for c in range(2):
        outputs[0][c] = probe_ref[c].T
    copies[1].wait()
    for n in range(intensity_ref.shape[1]):
        outputs[1][n] = intensity_ref[0, n].T
    for copy in copies[2:]:
        copy.wait()


def main_kernel(ring, window, position_ref, probe_ref, intensity_ref, table_ref, *rest):
    direct_ref, inverse_ref, forth_ref, back_ref = (table_ref.at[i] for i in range(4))
    unit_refs, rest = rest[: 4 * ring], rest[4 * ring :]
    keep_refs, send_refs, scratch = rest[: 2 * ring], rest[2 * ring : -5], rest[-5:]
    field_ref, wave_ref, patch_ref, total_ref, first_total_ref = scratch
    count = position_ref.shape[1]
    assemble(unit_refs, field_ref, ring, window)
    total_ref[...] = jnp.zeros_like(total_ref)
    first_total_ref[...] = jnp.zeros_like(first_total_ref)
    probe_re, probe_im = probe_ref[0], probe_ref[1]
    exits = []
    for n in range(count):
        re, im = cut(field_ref, 0, position_ref, n, window)
        exits.append((probe_re * re - probe_im * im, probe_re * im + probe_im * re))
    for n in range(count):
        patch_ref[n, 0], patch_ref[n, 1] = cut(field_ref, 1, position_ref, n, window)
    waves = transform(exits, forth_ref, back_ref, window)
    exits = []
    for n in range(count):
        re, im = patch_ref[n, 0], patch_ref[n, 1]
        w_re, w_im = waves[n]
        wave_ref[n, 0] = w_re
        wave_ref[n, 1] = w_im
        exits.append((w_re * re - w_im * im, w_re * im + w_im * re))
    scaled = []
    for n, (re, im) in enumerate(transform(exits, direct_ref, inverse_ref, window)):
        misfit = re * re + im * im - intensity_ref[n]
        scaled.append((misfit * re, misfit * im))
    carried, gradients = [], []
    for n, (b_re, b_im) in enumerate(transform(scaled, inverse_ref, direct_ref, window)):
        w_re, w_im = wave_ref[n, 0], wave_ref[n, 1]
        p_re, p_im = patch_ref[n, 0], patch_ref[n, 1]
        carried.append((p_re * b_re + p_im * b_im, p_re * b_im - p_im * b_re))
        deposit(total_ref, position_ref, n, (w_re * b_re + w_im * b_im, w_re * b_im - w_im * b_re), window)
    hand_out(total_ref, 1, keep_refs, send_refs, ring, window)
    for n, (b_re, b_im) in enumerate(transform(carried, back_ref, forth_ref, window)):
        gradient = (probe_re * b_re + probe_im * b_im, probe_re * b_im - probe_im * b_re)
        deposit(first_total_ref, position_ref, n, gradient, window)
    hand_out(first_total_ref, 0, keep_refs, send_refs, ring, window)


def sum_kernel(scale, *refs):
    total = refs[0][...]
    for ref in refs[1:-1]:
        total += ref[...]
    refs[-1][...] = total * scale


VMEM = pl.BlockSpec(memory_space=pltpu.VMEM)
HBM = pl.BlockSpec(memory_space=pltpu.HBM)
SMEM = pl.BlockSpec(memory_space=pltpu.SMEM)
PARAMS = pltpu.CompilerParams(vmem_limit_bytes=40 << 20)


def cost(flops, moved):
    return pl.CostEstimate(flops=flops, bytes_accessed=moved, transcendentals=0)


def body(object_slices, probe, intensity, positions):
    layers, _, rows, width = object_slices.shape
    window = probe.shape[1]
    count = positions.shape[1]
    regions = lax.axis_size("region")
    devices = lax.axis_size("probe")
    ring = devices // CORES
    columns = devices * width
    table = jnp.asarray(tables(window))
    unit = jax.ShapeDtypeStruct((layers, 2, width, rows), jnp.float32)
    field = pltpu.VMEM((layers, 2, 2, columns + window, rows), jnp.float32)
    total = pltpu.VMEM((2, 2, columns + window, rows), jnp.float32)
    wave_scratch = pltpu.VMEM((count, 2, window, window), jnp.float32)
    dft_flops = count * 2 * 3 * 2 * window * (2 * window) ** 2

    def swap(value):
        return lax.ppermute(value, "probe", [(i, i ^ 1) for i in range(devices)])

    def route(step, band):
        pairs = []
        for r in range(regions):
            for d in range(devices):
                there = ((d // CORES + step) % ring) * CORES + d % CORES
                pairs.append((r * devices + d, ((r + band) % regions) * devices + there))
        return pairs

    def fetch(value, step, band):
        return lax.ppermute(value, ("region", "probe"), [(b, a) for a, b in route(step, band)])

    def give(value, step, band):
        return lax.ppermute(value, ("region", "probe"), route(step, band))

    steps = travel_order(ring)
    tile = jnp.swapaxes(object_slices, 2, 3)
    probe_t, intensity_t, table = pl.pallas_call(
        prepare_kernel,
        out_shape=[
            jax.ShapeDtypeStruct(probe.shape, jnp.float32),
            jax.ShapeDtypeStruct(intensity.shape[1:], jnp.float32),
            jax.ShapeDtypeStruct(table.shape, table.dtype),
        ],
        in_specs=[HBM] * 3,
        out_specs=[VMEM] * 3,
        scratch_shapes=[
            pltpu.VMEM(probe.shape, jnp.float32),
            pltpu.VMEM(intensity.shape, jnp.float32),
            pltpu.SemaphoreType.DMA((3,)),
        ],
        compiler_params=PARAMS,
        cost_estimate=cost(1, 1),
    )(*(pltpu.with_memory_space_constraint(value, pltpu.HBM) for value in (probe, intensity, table)))
    early = [at for at, step in enumerate(steps) if all(step)]
    late = [at for at, step in enumerate(steps) if at and not all(step)]
    arrived = {at: fetch(tile, *steps[at]) for at in early + late}
    values, probe_t = lax.optimization_barrier(([arrived[at] for at in early], probe_t))
    arrived[0] = tile
    arrived.update(zip(early, values))
    swapped = {at: swap(arrived[at]) for at in [0] + early}
    values = lax.optimization_barrier(([arrived[at] for at in late], [swapped[at] for at in early]))
    arrived.update(zip(late, values[0]))
    swapped.update(zip(early, values[1]))
    swapped.update({at: swap(arrived[at]) for at in late})
    gathered = [value for at in range(len(steps)) for value in (arrived[at], swapped[at])]
    outputs = pl.pallas_call(
        lambda *refs: main_kernel(ring, window, *refs),
        out_shape=[unit] * (2 * len(steps)),
        in_specs=[SMEM] + [VMEM] * (3 + 4 * ring),
        out_specs=[VMEM] * (2 * len(steps)),
        scratch_shapes=[field, wave_scratch, wave_scratch, total, total],
        compiler_params=PARAMS,
        cost_estimate=cost(4 * dft_flops, 8 << 20),
    )(positions, probe_t, intensity_t, table, *gathered)
    keep, send = outputs[: len(steps)], outputs[len(steps) :]
    order = early + late[::-1]
    other = {at: swap(send[at]) for at in order}
    own, other[order[0]] = lax.optimization_barrier((send[0], other[order[0]]))
    terms = [give(keep[at] + other[at], *steps[at]) for at in order]
    other_own = swap(own)
    gradient = pl.pallas_call(
        lambda *refs: sum_kernel(1.0 / (count * devices), *refs),
        out_shape=unit,
        in_specs=[VMEM] * (len(steps) + 1),
        out_specs=VMEM,
        compiler_params=PARAMS,
    )(keep[0], other_own, *terms)
    return jnp.swapaxes(gradient, 2, 3)


def solution(mesh):
    placed = (
        P("group", None, "region", "probe"),
        P("group", None, None),
        P("region", "probe", "group", None),
        P("region", "probe", "group"),
    )
    return jax.shard_map(
        body,
        mesh=mesh,
        in_specs=placed,
        out_specs=P("group", None, "region", "probe"),
        check_vma=False,
    )
```

```python
import math

import jax
import jax.numpy as jnp
import ml_dtypes
import numpy as np
from jax import lax
from jax.experimental import pallas as pl
from jax.experimental.pallas import tpu as pltpu
from jax.sharding import PartitionSpec as P

CORES = 2
PAIRED = 2
HALF = 64


def split_table(table):
    high = table.astype(ml_dtypes.bfloat16)
    low = (table - high.astype(np.float64)).astype(ml_dtypes.bfloat16)
    return np.stack([high, low])


def as_real(table):
    return np.block([[table.real, table.imag], [-table.imag, table.real]])


def tables(window):
    indices = np.arange(window)
    angles = 2.0 * math.pi * ((indices[:, None] * indices[None, :]) % window) / window
    transform = np.exp(-1j * angles) / math.sqrt(window)
    frequency = np.where(indices < window // 2, indices, indices - window) / window
    step = (transform.conj() * np.exp(-60j * frequency**2)) @ transform
    step = (step + step.T) / 2
    return np.stack([split_table(as_real(m)) for m in (transform, transform.conj(), step, step.conj())])


def split(values):
    high = values.astype(jnp.bfloat16)
    low = (values - high.astype(jnp.float32)).astype(jnp.bfloat16)
    return high, low


def times_right(values, table_ref):
    high, low = split(values)
    rows = values.shape[0]
    both = jnp.dot(jnp.concatenate([high, low], axis=0), table_ref[0], preferred_element_type=jnp.float32)
    return both[:rows] + both[rows:] + jnp.dot(high, table_ref[1], preferred_element_type=jnp.float32)


def times_left(table_ref, values):
    high, low = split(values)
    rows = values.shape[0]
    both = jnp.dot(jnp.concatenate([table_ref[0], table_ref[1]], axis=0), high, preferred_element_type=jnp.float32)
    return both[:rows] + both[rows:] + jnp.dot(table_ref[0], low, preferred_element_type=jnp.float32)


def transform(pairs, right_ref, left_ref, window):
    halves = []
    for at in range(0, len(pairs), PAIRED):
        group = pairs[at : at + PAIRED]
        rows = [jnp.concatenate([pair[c] for pair in group], axis=1) for c in range(2)]
        whole = times_left(left_ref, jnp.concatenate(rows, axis=0))
        for n in range(len(group)):
            columns = slice(n * window, (n + 1) * window)
            halves.append(jnp.concatenate([whole[:window, columns], whole[window:, columns]], axis=1))
    outs = [times_right(half, right_ref) for half in halves]
    return [(out[:, :window], out[:, window:]) for out in outs]


def travel_order(ring):
    return [(0, 0), (0, 1)] + [(step, band) for band in range(2) for step in range(1, ring)]


def assemble(unit_refs, field_ref, ring, window):
    me = lax.axis_index("probe")
    x, core = me // CORES, me % CORES
    layers = field_ref.shape[0]
    columns = field_ref.shape[3] - window
    at = 0
    for step, band in travel_order(ring):
        tile = lax.rem(x + step, ring)
        for owner in (core, 1 - core):
            where = pl.ds(pl.multiple_of((tile * CORES + owner) * HALF, HALF), HALF)
            for layer in range(layers):
                for c in range(2):
                    field_ref[layer, c, band, where, :] = unit_refs[at][layer, c]
            at += 1
    field_ref[:, :, :, columns:, :] = field_ref[:, :, :, :window, :]


def cut(field_ref, layer, position_ref, n, window):
    row, column = position_ref[0, n, 0], position_ref[0, n, 1]
    back = lax.rem(window - row, window)
    lane = lax.broadcasted_iota(jnp.int32, (window, window), 1)
    halves = []
    for c in range(2):
        first = pltpu.roll(field_ref[layer, c, 0, pl.ds(column, window), :], back, 1)
        second = pltpu.roll(field_ref[layer, c, 1, pl.ds(column, window), :], back, 1)
        halves.append(jnp.where(lane < window - row, first, second))
    return tuple(halves)


def deposit(total_ref, position_ref, n, pair, window):
    row, column = position_ref[0, n, 0], position_ref[0, n, 1]
    lane = lax.broadcasted_iota(jnp.int32, (window, window), 1)
    where = pl.ds(column, window)
    for c in range(2):
        turned = pltpu.roll(pair[c], row, 1)
        total_ref[c, 0, where, :] += jnp.where(lane >= row, turned, 0.0)
        total_ref[c, 1, where, :] += jnp.where(lane < row, turned, 0.0)


def hand_out(total_ref, layer, keep_refs, send_refs, ring, window):
    me = lax.axis_index("probe")
    x, core = me // CORES, me % CORES
    columns = total_ref.shape[2] - window
    total_ref[:, :, :window, :] += total_ref[:, :, columns:, :]
    for at, (step, band) in enumerate(travel_order(ring)):
        tile = lax.rem(x + step, ring)
        for owner, ref in ((core, keep_refs[at]), (1 - core, send_refs[at])):
            where = pl.ds(pl.multiple_of((tile * CORES + owner) * HALF, HALF), HALF)
            for c in range(2):
                ref[layer, c] = total_ref[c, band, where, :]


def prepare_kernel(*refs):
    sources, outputs = refs[:3], refs[3:6]
    probe_ref, intensity_ref, sems = refs[6:]
    targets = (probe_ref, intensity_ref) + outputs[2:]
    copies = [pltpu.make_async_copy(a, b, sems.at[i]) for i, (a, b) in enumerate(zip(sources, targets))]
    for copy in copies:
        copy.start()
    copies[0].wait()
    for c in range(2):
        outputs[0][c] = probe_ref[c].T
    copies[1].wait()
    for n in range(intensity_ref.shape[1]):
        outputs[1][n] = intensity_ref[0, n].T
    for copy in copies[2:]:
        copy.wait()


def main_kernel(ring, window, position_ref, probe_ref, intensity_ref, table_ref, *rest):
    direct_ref, inverse_ref, forth_ref, back_ref = (table_ref.at[i] for i in range(4))
    unit_refs, rest = rest[: 4 * ring], rest[4 * ring :]
    keep_refs, send_refs, (field_ref, wave_ref, total_ref, first_total_ref) = rest[: 2 * ring], rest[2 * ring : -4], rest[-4:]
    count = position_ref.shape[1]
    assemble(unit_refs, field_ref, ring, window)
    total_ref[...] = jnp.zeros_like(total_ref)
    first_total_ref[...] = jnp.zeros_like(first_total_ref)
    probe_re, probe_im = probe_ref[0], probe_ref[1]
    exits = []
    for n in range(count):
        re, im = cut(field_ref, 0, position_ref, n, window)
        exits.append((probe_re * re - probe_im * im, probe_re * im + probe_im * re))
    waves = transform(exits, forth_ref, back_ref, window)
    exits = []
    for n in range(count):
        re, im = cut(field_ref, 1, position_ref, n, window)
        w_re, w_im = waves[n]
        wave_ref[n, 0] = w_re
        wave_ref[n, 1] = w_im
        exits.append((w_re * re - w_im * im, w_re * im + w_im * re))
    scaled = []
    for n, (re, im) in enumerate(transform(exits, direct_ref, inverse_ref, window)):
        misfit = re * re + im * im - intensity_ref[n]
        scaled.append((misfit * re, misfit * im))
    carried, gradients = [], []
    for n, (b_re, b_im) in enumerate(transform(scaled, inverse_ref, direct_ref, window)):
        w_re, w_im = wave_ref[n, 0], wave_ref[n, 1]
        p_re, p_im = cut(field_ref, 1, position_ref, n, window)
        carried.append((p_re * b_re + p_im * b_im, p_re * b_im - p_im * b_re))
        deposit(total_ref, position_ref, n, (w_re * b_re + w_im * b_im, w_re * b_im - w_im * b_re), window)
    hand_out(total_ref, 1, keep_refs, send_refs, ring, window)
    for n, (b_re, b_im) in enumerate(transform(carried, back_ref, forth_ref, window)):
        gradient = (probe_re * b_re + probe_im * b_im, probe_re * b_im - probe_im * b_re)
        deposit(first_total_ref, position_ref, n, gradient, window)
    hand_out(first_total_ref, 0, keep_refs, send_refs, ring, window)


def sum_kernel(scale, *refs):
    inputs, (out_ref, total_ref, sems) = refs[:-3], refs[-3:]
    copies = []
    for layer in range(out_ref.shape[0]):
        total = inputs[0][layer]
        for ref in inputs[1:]:
            total += ref[layer]
        total_ref[layer] = total * scale
        copies.append(pltpu.make_async_copy(total_ref.at[layer], out_ref.at[layer], sems.at[layer]))
        copies[-1].start()
    for copy in copies:
        copy.wait()


VMEM = pl.BlockSpec(memory_space=pltpu.VMEM)
HBM = pl.BlockSpec(memory_space=pltpu.HBM)
SMEM = pl.BlockSpec(memory_space=pltpu.SMEM)
PARAMS = pltpu.CompilerParams(vmem_limit_bytes=40 << 20)


def cost(flops, moved):
    return pl.CostEstimate(flops=flops, bytes_accessed=moved, transcendentals=0)


def body(object_slices, probe, intensity, positions):
    layers, _, rows, width = object_slices.shape
    window = probe.shape[1]
    count = positions.shape[1]
    regions = lax.axis_size("region")
    devices = lax.axis_size("probe")
    ring = devices // CORES
    columns = devices * width
    table = jnp.asarray(tables(window))
    unit = jax.ShapeDtypeStruct((layers, 2, width, rows), jnp.float32)
    field = pltpu.VMEM((layers, 2, 2, columns + window, rows), jnp.float32)
    total = pltpu.VMEM((2, 2, columns + window, rows), jnp.float32)
    wave_scratch = pltpu.VMEM((count, 2, window, window), jnp.float32)
    dft_flops = count * 2 * 3 * 2 * window * (2 * window) ** 2

    def swap(value):
        return lax.ppermute(value, "probe", [(i, i ^ 1) for i in range(devices)])

    def route(step, band):
        pairs = []
        for r in range(regions):
            for d in range(devices):
                there = ((d // CORES + step) % ring) * CORES + d % CORES
                pairs.append((r * devices + d, ((r + band) % regions) * devices + there))
        return pairs

    def fetch(value, step, band):
        return lax.ppermute(value, ("region", "probe"), [(b, a) for a, b in route(step, band)])

    def give(value, step, band):
        return lax.ppermute(value, ("region", "probe"), route(step, band))

    steps = travel_order(ring)
    tile = jnp.swapaxes(object_slices, 2, 3)
    probe_t, intensity_t, table = pl.pallas_call(
        prepare_kernel,
        out_shape=[
            jax.ShapeDtypeStruct(probe.shape, jnp.float32),
            jax.ShapeDtypeStruct(intensity.shape[1:], jnp.float32),
            jax.ShapeDtypeStruct(table.shape, table.dtype),
        ],
        in_specs=[HBM] * 3,
        out_specs=[VMEM] * 3,
        scratch_shapes=[
            pltpu.VMEM(probe.shape, jnp.float32),
            pltpu.VMEM(intensity.shape, jnp.float32),
            pltpu.SemaphoreType.DMA((3,)),
        ],
        compiler_params=PARAMS,
        cost_estimate=cost(1, 1),
    )(*(pltpu.with_memory_space_constraint(value, pltpu.HBM) for value in (probe, intensity, table)))
    early = [at for at, step in enumerate(steps) if all(step)]
    late = [at for at, step in enumerate(steps) if at and not all(step)]
    arrived = {at: fetch(tile, *steps[at]) for at in early + late}
    values, probe_t = lax.optimization_barrier(([arrived[at] for at in early], probe_t))
    arrived[0] = tile
    arrived.update(zip(early, values))
    swapped = {at: swap(arrived[at]) for at in [0] + early}
    values = lax.optimization_barrier(([arrived[at] for at in late], [swapped[at] for at in early]))
    arrived.update(zip(late, values[0]))
    swapped.update(zip(early, values[1]))
    swapped.update({at: swap(arrived[at]) for at in late})
    gathered = [value for at in range(len(steps)) for value in (arrived[at], swapped[at])]
    outputs = pl.pallas_call(
        lambda *refs: main_kernel(ring, window, *refs),
        out_shape=[unit] * (2 * len(steps)),
        in_specs=[SMEM] + [VMEM] * (3 + 4 * ring),
        out_specs=[VMEM] * (2 * len(steps)),
        scratch_shapes=[field, wave_scratch, total, total],
        compiler_params=PARAMS,
        cost_estimate=cost(4 * dft_flops, 8 << 20),
    )(positions, probe_t, intensity_t, table, *gathered)
    keep, send = outputs[: len(steps)], outputs[len(steps) :]
    order = early + late
    other = {at: swap(send[at]) for at in order}
    own, other[order[0]] = lax.optimization_barrier((send[0], other[order[0]]))
    terms = [give(keep[at] + other[at], *steps[at]) for at in order]
    other_own = swap(own)
    gradient = pl.pallas_call(
        lambda *refs: sum_kernel(1.0 / (count * devices), *refs),
        out_shape=unit,
        in_specs=[VMEM] * (len(steps) + 1),
        out_specs=HBM,
        scratch_shapes=[pltpu.VMEM(unit.shape, jnp.float32), pltpu.SemaphoreType.DMA((layers,))],
        compiler_params=PARAMS,
    )(keep[0], other_own, *terms)
    return jnp.swapaxes(gradient, 2, 3)


def solution(mesh):
    placed = (
        P("group", None, "region", "probe"),
        P("group", None, None),
        P("region", "probe", "group", None),
        P("region", "probe", "group"),
    )
    return jax.shard_map(
        body,
        mesh=mesh,
        in_specs=placed,
        out_specs=P("group", None, "region", "probe"),
        check_vma=False,
    )
```

```python
import math

import jax
import jax.numpy as jnp
import ml_dtypes
import numpy as np
from jax import lax
from jax.experimental import pallas as pl
from jax.experimental.pallas import tpu as pltpu
from jax.sharding import PartitionSpec as P

CORES = 2
PAIRED = 4
HALF = 64


def split_table(table):
    high = table.astype(ml_dtypes.bfloat16)
    low = (table - high.astype(np.float64)).astype(ml_dtypes.bfloat16)
    return np.stack([high, low])


def as_real(table):
    return np.block([[table.real, table.imag], [-table.imag, table.real]])


def tables(window):
    indices = np.arange(window)
    angles = 2.0 * math.pi * ((indices[:, None] * indices[None, :]) % window) / window
    transform = np.exp(-1j * angles) / math.sqrt(window)
    frequency = np.where(indices < window // 2, indices, indices - window) / window
    step = (transform.conj() * np.exp(-60j * frequency**2)) @ transform
    step = (step + step.T) / 2
    return np.stack([split_table(as_real(m)) for m in (transform, transform.conj(), step, step.conj())])


def split(values):
    high = values.astype(jnp.bfloat16)
    low = (values - high.astype(jnp.float32)).astype(jnp.bfloat16)
    return high, low


def times_right(values, table_ref):
    high, low = split(values)
    rows = values.shape[0]
    both = jnp.dot(jnp.concatenate([high, low], axis=0), table_ref[0], preferred_element_type=jnp.float32)
    return both[:rows] + both[rows:] + jnp.dot(high, table_ref[1], preferred_element_type=jnp.float32)


def times_left(table_ref, values):
    high, low = split(values)
    rows = values.shape[0]
    both = jnp.dot(jnp.concatenate([table_ref[0], table_ref[1]], axis=0), high, preferred_element_type=jnp.float32)
    return both[:rows] + both[rows:] + jnp.dot(table_ref[0], low, preferred_element_type=jnp.float32)


def transform(pairs, right_ref, left_ref, window):
    halves = []
    for at in range(0, len(pairs), PAIRED):
        group = pairs[at : at + PAIRED]
        rows = [jnp.concatenate([pair[c] for pair in group], axis=1) for c in range(2)]
        whole = times_left(left_ref, jnp.concatenate(rows, axis=0))
        for n in range(len(group)):
            columns = slice(n * window, (n + 1) * window)
            halves.append(jnp.concatenate([whole[:window, columns], whole[window:, columns]], axis=1))
    outs = [times_right(half, right_ref) for half in halves]
    return [(out[:, :window], out[:, window:]) for out in outs]


def travel_order(ring):
    return [(0, 0), (0, 1)] + [(step, band) for band in range(2) for step in range(1, ring)]


def assemble(unit_refs, field_ref, ring, window):
    me = lax.axis_index("probe")
    x, core = me // CORES, me % CORES
    layers = field_ref.shape[0]
    columns = field_ref.shape[3] - window
    at = 0
    for step, band in travel_order(ring):
        tile = lax.rem(x + step, ring)
        for owner in (core, 1 - core):
            where = pl.ds(pl.multiple_of((tile * CORES + owner) * HALF, HALF), HALF)
            for layer in range(layers):
                for c in range(2):
                    field_ref[layer, c, band, where, :] = unit_refs[at][layer, c]
            at += 1
    field_ref[:, :, :, columns:, :] = field_ref[:, :, :, :window, :]


def cut(field_ref, layer, position_ref, n, window):
    row, column = position_ref[0, n, 0], position_ref[0, n, 1]
    back = lax.rem(window - row, window)
    lane = lax.broadcasted_iota(jnp.int32, (window, window), 1)
    halves = []
    for c in range(2):
        first = pltpu.roll(field_ref[layer, c, 0, pl.ds(column, window), :], back, 1)
        second = pltpu.roll(field_ref[layer, c, 1, pl.ds(column, window), :], back, 1)
        halves.append(jnp.where(lane < window - row, first, second))
    return tuple(halves)


def deposit(total_ref, position_ref, n, pair, window):
    row, column = position_ref[0, n, 0], position_ref[0, n, 1]
    lane = lax.broadcasted_iota(jnp.int32, (window, window), 1)
    where = pl.ds(column, window)
    for c in range(2):
        turned = pltpu.roll(pair[c], row, 1)
        total_ref[c, 0, where, :] += jnp.where(lane >= row, turned, 0.0)
        total_ref[c, 1, where, :] += jnp.where(lane < row, turned, 0.0)


def hand_out(total_ref, layer, keep_refs, send_refs, ring, window):
    me = lax.axis_index("probe")
    x, core = me // CORES, me % CORES
    columns = total_ref.shape[2] - window
    total_ref[:, :, :window, :] += total_ref[:, :, columns:, :]
    for at, (step, band) in enumerate(travel_order(ring)):
        tile = lax.rem(x + step, ring)
        for owner, ref in ((core, keep_refs[at]), (1 - core, send_refs[at])):
            where = pl.ds(pl.multiple_of((tile * CORES + owner) * HALF, HALF), HALF)
            for c in range(2):
                ref[layer, c] = total_ref[c, band, where, :]


def prepare_kernel(*refs):
    sources, outputs = refs[:3], refs[3:6]
    probe_ref, intensity_ref, sems = refs[6:]
    targets = (probe_ref, intensity_ref) + outputs[2:]
    copies = [pltpu.make_async_copy(a, b, sems.at[i]) for i, (a, b) in enumerate(zip(sources, targets))]
    for copy in copies:
        copy.start()
    copies[0].wait()
    for c in range(2):
        outputs[0][c] = probe_ref[c].T
    copies[1].wait()
    for n in range(intensity_ref.shape[1]):
        outputs[1][n] = intensity_ref[0, n].T
    for copy in copies[2:]:
        copy.wait()


def main_kernel(ring, window, position_ref, probe_ref, intensity_ref, table_ref, *rest):
    direct_ref, inverse_ref, forth_ref, back_ref = (table_ref.at[i] for i in range(4))
    unit_refs, rest = rest[: 4 * ring], rest[4 * ring :]
    keep_refs, send_refs, (field_ref, wave_ref, total_ref, first_total_ref) = rest[: 2 * ring], rest[2 * ring : -4], rest[-4:]
    count = position_ref.shape[1]
    assemble(unit_refs, field_ref, ring, window)
    total_ref[...] = jnp.zeros_like(total_ref)
    first_total_ref[...] = jnp.zeros_like(first_total_ref)
    probe_re, probe_im = probe_ref[0], probe_ref[1]
    exits = []
    for n in range(count):
        re, im = cut(field_ref, 0, position_ref, n, window)
        exits.append((probe_re * re - probe_im * im, probe_re * im + probe_im * re))
    waves = transform(exits, forth_ref, back_ref, window)
    exits = []
    for n in range(count):
        re, im = cut(field_ref, 1, position_ref, n, window)
        w_re, w_im = waves[n]
        wave_ref[n, 0] = w_re
        wave_ref[n, 1] = w_im
        exits.append((w_re * re - w_im * im, w_re * im + w_im * re))
    scaled = []
    for n, (re, im) in enumerate(transform(exits, direct_ref, inverse_ref, window)):
        misfit = re * re + im * im - intensity_ref[n]
        scaled.append((misfit * re, misfit * im))
    carried, gradients = [], []
    for n, (b_re, b_im) in enumerate(transform(scaled, inverse_ref, direct_ref, window)):
        w_re, w_im = wave_ref[n, 0], wave_ref[n, 1]
        p_re, p_im = cut(field_ref, 1, position_ref, n, window)
        carried.append((p_re * b_re + p_im * b_im, p_re * b_im - p_im * b_re))
        deposit(total_ref, position_ref, n, (w_re * b_re + w_im * b_im, w_re * b_im - w_im * b_re), window)
    hand_out(total_ref, 1, keep_refs, send_refs, ring, window)
    for n, (b_re, b_im) in enumerate(transform(carried, back_ref, forth_ref, window)):
        gradient = (probe_re * b_re + probe_im * b_im, probe_re * b_im - probe_im * b_re)
        deposit(first_total_ref, position_ref, n, gradient, window)
    hand_out(first_total_ref, 0, keep_refs, send_refs, ring, window)


def sum_kernel(scale, *refs):
    inputs, (out_ref, total_ref, sems) = refs[:-3], refs[-3:]
    copies = []
    for layer in range(out_ref.shape[0]):
        total = inputs[0][layer]
        for ref in inputs[1:]:
            total += ref[layer]
        total_ref[layer] = total * scale
        copies.append(pltpu.make_async_copy(total_ref.at[layer], out_ref.at[layer], sems.at[layer]))
        copies[-1].start()
    for copy in copies:
        copy.wait()


VMEM = pl.BlockSpec(memory_space=pltpu.VMEM)
HBM = pl.BlockSpec(memory_space=pltpu.HBM)
SMEM = pl.BlockSpec(memory_space=pltpu.SMEM)
PARAMS = pltpu.CompilerParams(vmem_limit_bytes=40 << 20)


def cost(flops, moved):
    return pl.CostEstimate(flops=flops, bytes_accessed=moved, transcendentals=0)


def body(object_slices, probe, intensity, positions):
    layers, _, rows, width = object_slices.shape
    window = probe.shape[1]
    count = positions.shape[1]
    regions = lax.axis_size("region")
    devices = lax.axis_size("probe")
    ring = devices // CORES
    columns = devices * width
    table = jnp.asarray(tables(window))
    unit = jax.ShapeDtypeStruct((layers, 2, width, rows), jnp.float32)
    field = pltpu.VMEM((layers, 2, 2, columns + window, rows), jnp.float32)
    total = pltpu.VMEM((2, 2, columns + window, rows), jnp.float32)
    wave_scratch = pltpu.VMEM((count, 2, window, window), jnp.float32)
    dft_flops = count * 2 * 3 * 2 * window * (2 * window) ** 2

    def swap(value):
        return lax.ppermute(value, "probe", [(i, i ^ 1) for i in range(devices)])

    def route(step, band):
        pairs = []
        for r in range(regions):
            for d in range(devices):
                there = ((d // CORES + step) % ring) * CORES + d % CORES
                pairs.append((r * devices + d, ((r + band) % regions) * devices + there))
        return pairs

    def fetch(value, step, band):
        return lax.ppermute(value, ("region", "probe"), [(b, a) for a, b in route(step, band)])

    def give(value, step, band):
        return lax.ppermute(value, ("region", "probe"), route(step, band))

    steps = travel_order(ring)
    tile = jnp.swapaxes(object_slices, 2, 3)
    probe_t, intensity_t, table = pl.pallas_call(
        prepare_kernel,
        out_shape=[
            jax.ShapeDtypeStruct(probe.shape, jnp.float32),
            jax.ShapeDtypeStruct(intensity.shape[1:], jnp.float32),
            jax.ShapeDtypeStruct(table.shape, table.dtype),
        ],
        in_specs=[HBM] * 3,
        out_specs=[VMEM] * 3,
        scratch_shapes=[
            pltpu.VMEM(probe.shape, jnp.float32),
            pltpu.VMEM(intensity.shape, jnp.float32),
            pltpu.SemaphoreType.DMA((3,)),
        ],
        compiler_params=PARAMS,
        cost_estimate=cost(1, 1),
    )(*(pltpu.with_memory_space_constraint(value, pltpu.HBM) for value in (probe, intensity, table)))
    early = [at for at, step in enumerate(steps) if all(step)]
    late = [at for at, step in enumerate(steps) if at and not all(step)]
    arrived = {at: fetch(tile, *steps[at]) for at in early + late}
    values, probe_t = lax.optimization_barrier(([arrived[at] for at in early], probe_t))
    arrived[0] = tile
    arrived.update(zip(early, values))
    swapped = {at: swap(arrived[at]) for at in [0] + early}
    values = lax.optimization_barrier(([arrived[at] for at in late], [swapped[at] for at in early]))
    arrived.update(zip(late, values[0]))
    swapped.update(zip(early, values[1]))
    swapped.update({at: swap(arrived[at]) for at in late})
    gathered = [value for at in range(len(steps)) for value in (arrived[at], swapped[at])]
    outputs = pl.pallas_call(
        lambda *refs: main_kernel(ring, window, *refs),
        out_shape=[unit] * (2 * len(steps)),
        in_specs=[SMEM] + [VMEM] * (3 + 4 * ring),
        out_specs=[VMEM] * (2 * len(steps)),
        scratch_shapes=[field, wave_scratch, total, total],
        compiler_params=PARAMS,
        cost_estimate=cost(4 * dft_flops, 8 << 20),
    )(positions, probe_t, intensity_t, table, *gathered)
    keep, send = outputs[: len(steps)], outputs[len(steps) :]
    order = early + late[::-1]
    other = {at: swap(send[at]) for at in order}
    own, other[order[0]] = lax.optimization_barrier((send[0], other[order[0]]))
    terms = [give(keep[at] + other[at], *steps[at]) for at in order]
    other_own = swap(own)
    gradient = pl.pallas_call(
        lambda *refs: sum_kernel(1.0 / (count * devices), *refs),
        out_shape=unit,
        in_specs=[VMEM] * (len(steps) + 1),
        out_specs=HBM,
        scratch_shapes=[pltpu.VMEM(unit.shape, jnp.float32), pltpu.SemaphoreType.DMA((layers,))],
        compiler_params=PARAMS,
    )(keep[0], other_own, *terms)
    return jnp.swapaxes(gradient, 2, 3)


def solution(mesh):
    placed = (
        P("group", None, "region", "probe"),
        P("group", None, None),
        P("region", "probe", "group", None),
        P("region", "probe", "group"),
    )
    return jax.shard_map(
        body,
        mesh=mesh,
        in_specs=placed,
        out_specs=P("group", None, "region", "probe"),
        check_vma=False,
    )
```
